32 devices in a mesh: scene: 4 (over y, core), frame: 8 (over z, x).
Axes of the slice: x: 2, y: 2, z: 4, core: 2. Of those that a mesh axis runs over, the one named last changes fastest.
Arguments:
- occupancy: bfloat16 [4, 32, 64, 2048], P('scene', 'frame'), may hold values from -6 to 6
- scene_lengths: int32 [4], P('scene'), may hold values from 8 to 32, as said below
- conv1_weight: bfloat16 [128, 1728], replicated, may hold values from -0.15625 to 0.15625
- conv2_weight: bfloat16 [256, 3456], replicated, may hold values from -0.109375 to 0.109375
- temporal_weight: bfloat16 [3, 256, 256], replicated, may hold values from -0.21875 to 0.21875
- query_weight: bfloat16 [256, 256], replicated
- key_weight: bfloat16 [256, 256], replicated
- value_weight: bfloat16 [256, 256], replicated, may hold values from -0.375 to 0.375
- out_weight: bfloat16 [256, 256], replicated, may hold values from -0.375 to 0.375
Outputs:
- encoded: bfloat16 [4, 32, 256, 512], P('scene', 'frame')
- kl_loss: float32 [], replicated
The draws below stay inside these ranges and needn't reach their ends.
Inputs may be any that keep to these rules, and one draw needn't show every extreme that they name: `scene_lengths`: non-decreasing along the scenes; the first scene has exactly 8 frames with data and the last exactly 32.
All inputs are finite; a program needn't handle non-finite values.
Results may differ from the reference program's by a relative error of at most 0.011.
Values may be sent and summed in bfloat16 or wider, within the bound.
No kernel may reach another device: no remote copies, remote signals or barrier semaphores. Data moves between devices by JAX's collectives and lax.ppermute only.
A program may use at most 192 MiB of HBM per device.

```python
import jax
import jax.numpy as jnp
from jax import lax

CIN = 64
C1 = 128
C2 = 256
HEADS = 4
HD = 64
HI = 16
ZD = 8
CELLS = 512
CELLS_IN = 2048
FRAMES = 32
SCENES = 4


def query_key_pair(key):
    base_key = jax.random.fold_in(key, 11)
    first_draw = jax.random.normal(jax.random.fold_in(base_key, 1), (C2, C2), jnp.float32) * C2 ** (-0.5)
    second_draw = jax.random.normal(jax.random.fold_in(base_key, 2), (C2, C2), jnp.float32) * C2 ** (-0.5)
    return (first_draw, second_draw)


def draw_query_weight(key, part):
    first_draw, second_draw = query_key_pair(key)
    return first_draw.astype(jnp.bfloat16)


def draw_key_weight(key, part):
    first_draw, second_draw = query_key_pair(key)
    return second_draw.astype(jnp.bfloat16)


def draw_scene_lengths(key, part):
    drawn = jax.random.randint(jax.random.fold_in(key, 3), (SCENES,), 8, FRAMES + 1)
    drawn = jnp.sort(drawn)
    drawn = drawn.at[0].set(8)
    drawn = drawn.at[SCENES - 1].set(FRAMES)
    return drawn.astype(jnp.int32)


def level_of(key, extent, cuts, low, top_value):
    def one(position, blocks):
        steps = jax.random.uniform(jax.random.fold_in(jax.random.fold_in(key, 6), position), (blocks,), jnp.float32, low / len(cuts), top_value / len(cuts))
        return jnp.repeat(jnp.exp(steps), extent[position] // blocks).reshape((-1,) + (1,) * (len(extent) - position - 1))

    factor_of = one(*cuts[0])
    for cut in cuts[1:]:
        factor_of = factor_of * one(*cut)
    return factor_of


def centred(key, dims, scale, reach, shards=(), kind=jnp.bfloat16):
    loudness = level_of(key, dims, shards, -0.22, 0.18) if shards else 1.0
    values = jax.random.normal(key, dims, jnp.float32) * scale * loudness
    return jnp.minimum(jnp.maximum(values, -reach), reach).astype(kind)


def setup_inputs(seed: int = 0) -> dict:
    key_of = jax.random.split(jax.random.key(seed), 10)
    occupancy = centred(key_of[0], (SCENES, FRAMES, CIN, CELLS_IN), 1.0, 6.0, ((0, 4), (1, 8)))
    scene_lengths = draw_scene_lengths(jax.random.fold_in(key_of[9], 71), 0)
    conv1_weight = centred(key_of[2], (C1, CIN * 27), (CIN * 27) ** -0.5, 0.15625)
    conv2_weight = centred(key_of[3], (C2, C1 * 27), (C1 * 27) ** -0.5, 0.109375)
    temporal_weight = centred(key_of[4], (3, C2, C2), (3 * C2) ** -0.5, 0.21875)
    query_weight = draw_query_weight(jax.random.fold_in(key_of[9], 71), 0)
    key_weight = draw_key_weight(jax.random.fold_in(key_of[9], 71), 0)
    value_weight = centred(key_of[7], (C2, C2), C2 ** -0.5, 0.375)
    out_weight = centred(key_of[8], (C2, C2), C2 ** -0.5, 0.375)
    return {"occupancy": occupancy, "scene_lengths": scene_lengths, "conv1_weight": conv1_weight, "conv2_weight": conv2_weight, "temporal_weight": temporal_weight, "query_weight": query_weight, "key_weight": key_weight, "value_weight": value_weight, "out_weight": out_weight}


NORM_EPS = 1e-06

def spatial_conv(voxels, weight, channels_in, stride):
    channels_out = weight.shape[0]
    kernel = weight.reshape(channels_out, channels_in, 3, 3, 3)
    return lax.conv_general_dilated(voxels, kernel, (stride, stride, 1), ((1, 1), (1, 1), (1, 1)), dimension_numbers=('NCDHW', 'OIDHW', 'NCDHW'), preferred_element_type=jnp.float32)

def mix_channels(weight, maps):
    return jnp.einsum('oc,fcn->fon', weight.astype(jnp.float32), maps.astype(jnp.float32))

def encode_scene(occupancy, length, conv1_weight, conv2_weight, temporal_weight, query_weight, key_weight, value_weight, out_weight):
    frames = occupancy.shape[0]
    voxels = occupancy.reshape(frames, CIN, HI, HI, ZD)
    first_maps = jax.nn.silu(spatial_conv(voxels, conv1_weight, CIN, 2)).astype(jnp.bfloat16)
    second_full = jax.nn.silu(spatial_conv(first_maps, conv2_weight, C1, 1))
    valid_rows = (jnp.arange(frames) < length).astype(jnp.float32)
    second_maps = (second_full.reshape(frames, C2, CELLS) * valid_rows[:, None, None]).astype(jnp.bfloat16)
    padded = jnp.pad(second_maps, ((1, 1), (0, 0), (0, 0)))
    temporal_sum = mix_channels(temporal_weight[0], padded[0:frames])
    temporal_sum = temporal_sum + mix_channels(temporal_weight[1], padded[1:frames + 1])
    temporal_sum = temporal_sum + mix_channels(temporal_weight[2], padded[2:frames + 2])
    residual_maps = (second_maps.astype(jnp.float32) + jax.nn.silu(temporal_sum)).astype(jnp.bfloat16)
    residual_f = residual_maps.astype(jnp.float32)
    normed = (residual_f * lax.rsqrt(lax.optimization_barrier(jnp.mean(residual_f * residual_f, axis=1, keepdims=True)) + NORM_EPS)).astype(jnp.bfloat16)
    queries = mix_channels(query_weight, normed).astype(jnp.bfloat16).reshape(frames, HEADS, HD, CELLS)
    key_rows = mix_channels(key_weight, normed).astype(jnp.bfloat16).reshape(frames, HEADS, HD, CELLS)
    value_rows = mix_channels(value_weight, normed).astype(jnp.bfloat16).reshape(frames, HEADS, HD, CELLS)
    scores = jnp.einsum('qhdc,khdc->qkhc', queries.astype(jnp.float32), key_rows.astype(jnp.float32)) * HD ** (-0.5)
    key_mask = (jnp.arange(frames) < length)[None, :, None, None]
    scores = jnp.where(key_mask, scores, -1e+30)
    row_max = lax.optimization_barrier(jnp.max(scores, axis=1, keepdims=True))
    raw_weights = jnp.where(key_mask, jnp.exp(scores - row_max), 0.0)
    row_total = lax.optimization_barrier(jnp.sum(raw_weights, axis=1))
    exp_weights = lax.optimization_barrier(raw_weights.astype(jnp.bfloat16))
    weighted = jnp.einsum('qkhc,khdc->qhdc', exp_weights.astype(jnp.float32), value_rows.astype(jnp.float32))
    attended = (weighted / row_total[:, :, None, :]).astype(jnp.bfloat16)
    out_full = residual_f + mix_channels(out_weight, attended.reshape(frames, C2, CELLS))
    return (out_full * valid_rows[:, None, None]).astype(jnp.bfloat16)

def reference(occupancy, scene_lengths, conv1_weight, conv2_weight, temporal_weight, query_weight, key_weight, value_weight, out_weight):

    def one_scene(pair_in):
        return encode_scene(pair_in[0], pair_in[1], conv1_weight, conv2_weight, temporal_weight, query_weight, key_weight, value_weight, out_weight)
    encoded = lax.map(one_scene, (occupancy, scene_lengths))
    grand_total = jnp.sum(jnp.square(encoded.astype(jnp.float32)))
    kl_loss = 0.5 * grand_total / float(SCENES * FRAMES * CELLS * C2)
    return (encoded, kl_loss)
```

```python
import functools

import jax
import jax.numpy as jnp
from jax import lax
from jax.experimental import pallas as pl
from jax.experimental.pallas import tpu as pltpu
from jax.sharding import PartitionSpec as P

CIN = 64
C1 = 128
C2 = 256
HEADS = 4
HD = 64
HI = 16
ZD = 8
CELLS = 512
ROWS = 8
ROW = 64
HALVES = 2
NORM_EPS = 1e-06
NEG = -1e30


def silu(v):
    half = 0.5 * v
    return half + half * jnp.tanh(half)


def shift_z(v, step):
    if step == 0:
        return v
    z = lax.broadcasted_iota(jnp.int32, v.shape, v.ndim - 2)
    moved = pltpu.roll(v, (-step) % ZD, v.ndim - 2)
    keep = (z + step >= 0) & (z + step < ZD)
    return jnp.where(keep, moved, 0.0)


def shift_w(v, step):
    if step == 0:
        return v
    zero = jnp.zeros_like(v[:1])
    if step < 0:
        return jnp.concatenate([zero, v[:-1]], axis=0)
    return jnp.concatenate([v[1:], zero], axis=0)


def conv_kernel(n, meta, occ, w1, w2, *rest):
    outs = rest[: HALVES * n]
    t1, t2, w1s, w2s, cols1, y1, cols2, y2, maps = rest[HALVES * n :]
    frames = occ.shape[0]
    me = meta[0]
    length = meta[1]
    bf16 = jnp.bfloat16

    for j in range(0, w1.shape[1], 128):
        width = min(128, w1.shape[1] - j)
        t1[j : j + width, :] = w1[:, j : j + width].astype(jnp.float32).T
    for half in range(2):
        for j in range(0, w2.shape[1], 128):
            t2[half, j : j + 128, :] = (
                w2[half * 128 : half * 128 + 128, j : j + 128].astype(jnp.float32).T
            )
    zero = jnp.zeros((CIN, C1), bf16)
    for kz in range(3):
        base = kz * 384

        def tap1(kh, kw):
            return t1[pl.ds(kh * 9 + kw * 3 + kz, CIN, stride=27), :].astype(bf16)

        for place, (kw, hp) in enumerate([(1, 0), (1, 1), (2, 0), (2, 1), (0, 0), (0, 1)]):
            rows = slice(base + place * CIN, base + place * CIN + CIN)
            w1s[rows, 0:C1] = tap1(hp + 1, kw)
            w1s[rows, C1 : 2 * C1] = tap1(0, kw) if hp == 1 else zero
    for kh in range(3):
        for kw in range(3):
            for kz in range(3):
                rows = slice((kw * 3 + kz) * C1, (kw * 3 + kz + 1) * C1)
                for half in range(2):
                    w2s[kh, rows, half * 128 : half * 128 + 128] = t2[
                        half, pl.ds(kh * 9 + kw * 3 + kz, C1, stride=27), :
                    ].astype(bf16)

    cols1[0:ROW, :] = jnp.zeros((ROW, cols1.shape[1]), bf16)
    cols2[0:ROW, :] = jnp.zeros((ROW, cols2.shape[1]), bf16)
    cols2[(ROWS + 1) * ROW :, :] = jnp.zeros((ROW, cols2.shape[1]), bf16)

    def frame(f, carry):
        for h in range(ROWS):
            upper = occ[f, :, h * 256 : h * 256 + 128]
            lower = occ[f, :, h * 256 + 128 : h * 256 + 256]
            tile = jnp.concatenate([upper, lower], axis=0).astype(jnp.float32).T
            tile = tile.reshape(8, 2, ZD, 128)
            even, odd = tile[:, 0], tile[:, 1]
            for kz in range(3):
                e, o = shift_z(even, kz - 1), shift_z(odd, kz - 1)
                parts = (e, o, shift_w(o, -1))
                for i, part in enumerate(parts):
                    lanes = slice(kz * 384 + i * 128, kz * 384 + i * 128 + 128)
                    cols1[(h + 1) * ROW : (h + 2) * ROW, lanes] = part.reshape(ROW, 128).astype(bf16)
        y1[...] = jnp.dot(cols1[...], w1s[...], preferred_element_type=jnp.float32)
        for h in range(ROWS):
            v = y1[(h + 1) * ROW : (h + 2) * ROW, 0:C1] + y1[h * ROW : (h + 1) * ROW, C1 : 2 * C1]
            v = silu(v).reshape(8, ZD, C1)
            for kz in range(3):
                moved = shift_z(v, kz - 1)
                for kw in range(3):
                    lanes = slice((kw * 3 + kz) * C1, (kw * 3 + kz + 1) * C1)
                    cols2[(h + 1) * ROW : (h + 2) * ROW, lanes] = (
                        shift_w(moved, kw - 1).reshape(ROW, C1).astype(bf16)
                    )
        acc = jnp.dot(cols2[0:CELLS, :], w2s[0], preferred_element_type=jnp.float32)
        acc = acc + jnp.dot(cols2[ROW : ROW + CELLS, :], w2s[1], preferred_element_type=jnp.float32)
        acc = acc + jnp.dot(
            cols2[2 * ROW : 2 * ROW + CELLS, :], w2s[2], preferred_element_type=jnp.float32
        )
        y2[...] = acc
        valid = jnp.where(me * frames + f < length, 1.0, 0.0)
        for h in range(ROWS):
            rows = slice(h * ROW, (h + 1) * ROW)
            maps[rows, :] = (silu(y2[rows, :]) * valid).astype(bf16)
        count = CELLS // (HALVES * n)
        for half in range(HALVES):
            for k in range(n):
                start = pl.multiple_of(half * (CELLS // HALVES) + (me ^ k) * count, count)
                outs[half * n + k][f] = maps[pl.ds(start, count), :]
        return carry

    lax.fori_loop(0, frames, frame, 0)


def conv_maps(n, meta, occ, w1, w2):
    frames = occ.shape[0]
    count = CELLS // (HALVES * n)
    vmem = pl.BlockSpec(memory_space=pltpu.VMEM)
    return pl.pallas_call(
        functools.partial(conv_kernel, n),
        out_shape=[jax.ShapeDtypeStruct((frames, count, C2), jnp.bfloat16)] * (HALVES * n),
        in_specs=[pl.BlockSpec(memory_space=pltpu.SMEM), vmem, vmem, vmem],
        out_specs=[vmem] * (HALVES * n),
        scratch_shapes=[
            pltpu.VMEM((CIN * 27, C1), jnp.float32),
            pltpu.VMEM((2, C1 * 27, 128), jnp.float32),
            pltpu.VMEM((1152, 2 * C1), jnp.bfloat16),
            pltpu.VMEM((3, 9 * C1, C2), jnp.bfloat16),
            pltpu.VMEM(((ROWS + 1) * ROW, 1152), jnp.bfloat16),
            pltpu.VMEM(((ROWS + 1) * ROW, 2 * C1), jnp.float32),
            pltpu.VMEM(((ROWS + 2) * ROW, 9 * C1), jnp.bfloat16),
            pltpu.VMEM((CELLS, C2), jnp.float32),
            pltpu.VMEM((CELLS, C2), jnp.bfloat16),
        ],
        cost_estimate=pl.CostEstimate(
            flops=2 * frames * CELLS * (C1 * CIN * 27 + C2 * C1 * 27),
            bytes_accessed=4_000_000,
            transcendentals=frames * CELLS * (C1 + C2),
        ),
    )(meta, occ, w1, w2)


def nt_dot(a, b):
    return lax.dot_general(a, b, (((1,), (1,)), ((), ())), preferred_element_type=jnp.float32)


def attend_kernel(n, meta, *rest):
    blocks = rest[:n]
    tw, wq, wk, wv, wo = rest[n : n + 5]
    outs = rest[n + 5 : 2 * n + 5]
    squares = rest[2 * n + 5]
    tws, seen, resid, q_s, k_s, v_s, att, bias, ones, p_s, vb = rest[2 * n + 6 :]
    me, length = meta[0], meta[1]
    frames, count = blocks[0].shape[0], blocks[0].shape[1]
    groups = count // 8
    total = n * frames
    rows = total * 8
    bf16 = jnp.bfloat16
    head_of = lax.broadcasted_iota(jnp.int32, (rows, C2), 1) // HD

    edge = jnp.zeros((groups, 1, 8, C2), jnp.float32)
    seen[:, 0:1] = edge
    seen[:, total + 1 : total + 2] = edge
    for k in range(n):
        first = (me ^ k) * frames + 1
        for f in range(frames):
            tile = blocks[k][f].astype(jnp.float32).reshape(groups, 8, C2)
            for g in range(groups):
                seen[g, first + f] = tile[g]

    at = lax.broadcasted_iota(jnp.int32, (rows, rows), 0)
    to = lax.broadcasted_iota(jnp.int32, (rows, rows), 1)
    bias[...] = jnp.where((at % 8 == to % 8) & (to // 8 < length), 0.0, NEG)
    for h in range(HEADS):
        ones[h * rows : (h + 1) * rows, :] = jnp.where(head_of == h, 1.0, 0.0).astype(bf16)
    squares[...] = jnp.zeros(squares.shape, jnp.float32)

    def group(g, carry):
        mix = jnp.concatenate(
            [seen[g, j : j + total].reshape(rows, C2).astype(bf16) for j in range(3)], axis=1
        )
        summed = jnp.zeros((rows, C2), jnp.float32)
        for j in range(3):
            summed = summed + nt_dot(mix[:, j * C2 : (j + 1) * C2], tw[j])
        here = seen[g, 1 : total + 1].reshape(rows, C2)
        res = (here + silu(summed)).astype(bf16).astype(jnp.float32)
        resid[...] = res
        mean = jnp.sum(res * res, axis=1, keepdims=True) * (1.0 / C2)
        normed = (res * lax.rsqrt(mean + NORM_EPS)).astype(bf16)
        q = (nt_dot(normed, wq[...]).astype(bf16) * HD ** (-0.5)).astype(bf16)
        keys = nt_dot(normed, wk[...]).astype(bf16)
        values = nt_dot(normed, wv[...]).astype(bf16)
        none = jnp.zeros((rows, C2), bf16)
        for h in range(HEADS):
            mine = head_of == h
            s = nt_dot(q, jnp.where(mine, keys, none)) + bias[...]
            top = jnp.max(s, axis=1, keepdims=True)
            p_s[:, h * rows : (h + 1) * rows] = jnp.exp(s - top).astype(bf16)
            vb[h * rows : (h + 1) * rows, :] = jnp.where(mine, values, none)
        weighted = jnp.dot(p_s[...], vb[...], preferred_element_type=jnp.float32)
        sums = jnp.dot(p_s[...], ones[...], preferred_element_type=jnp.float32)
        attended = (weighted / sums).astype(bf16)
        full = resid[...] + nt_dot(attended, wo[...])
        t = lax.broadcasted_iota(jnp.int32, (rows, C2), 0) // 8
        full = jnp.where(t < length, full, 0.0).astype(bf16).astype(jnp.float32)
        att[g] = full.reshape(total, 8, C2)
        sq = full * full
        squares[...] = squares[...] + jnp.sum(sq.reshape(total, 8, C2), axis=0)
        return carry

    lax.fori_loop(0, groups, group, 0)
    for k in range(n):
        first = (me ^ k) * frames
        for f in range(frames):
            tile = jnp.concatenate([att[g, first + f] for g in range(groups)], axis=0)
            outs[k][f] = tile.astype(bf16)


def attend(n, meta, blocks, tw, wq, wk, wv, wo):
    frames, count, _ = blocks[0].shape
    total = n * frames
    rows = total * 8
    groups = count // 8
    vmem = pl.BlockSpec(memory_space=pltpu.VMEM)
    res = pl.pallas_call(
        functools.partial(attend_kernel, n),
        out_shape=[jax.ShapeDtypeStruct(blocks[0].shape, jnp.bfloat16)] * n
        + [jax.ShapeDtypeStruct((8, C2), jnp.float32)],
        in_specs=[pl.BlockSpec(memory_space=pltpu.SMEM)] + [vmem] * (n + 5),
        out_specs=[vmem] * (n + 1),
        scratch_shapes=[
            pltpu.VMEM((8, 128), jnp.bfloat16),
            pltpu.VMEM((groups, total + 2, 8, C2), jnp.float32),
            pltpu.VMEM((rows, C2), jnp.float32),
            pltpu.VMEM((rows, C2), jnp.bfloat16),
            pltpu.VMEM((rows, C2), jnp.bfloat16),
            pltpu.VMEM((rows, C2), jnp.bfloat16),
            pltpu.VMEM((groups, total, 8, C2), jnp.float32),
            pltpu.VMEM((rows, rows), jnp.float32),
            pltpu.VMEM((HEADS * rows, C2), jnp.bfloat16),
            pltpu.VMEM((rows, HEADS * rows), jnp.bfloat16),
            pltpu.VMEM((HEADS * rows, C2), jnp.bfloat16),
        ],
        cost_estimate=pl.CostEstimate(
            flops=2 * groups * rows * C2 * (7 * C2 + 12 * rows),
            bytes_accessed=4_000_000,
            transcendentals=groups * rows * HEADS * rows,
        ),
    )(meta, *blocks, tw, wq, wk, wv, wo)
    return res[:n], res[n]


def gather_kernel(n, meta, *rest):
    blocks = rest[: HALVES * n]
    out = rest[HALVES * n]
    whole = rest[HALVES * n + 1]
    me = meta[0]
    frames, count = blocks[0].shape[0], blocks[0].shape[1]
    for half in range(HALVES):
        for k in range(n):
            start = pl.multiple_of(half * (CELLS // HALVES) + (me ^ k) * count, count)
            for f in range(frames):
                whole[f, pl.ds(start, count), :] = blocks[half * n + k][f]
    for f in range(frames):
        out[f] = whole[f].astype(jnp.float32).T.astype(jnp.bfloat16)


def gather(n, meta, blocks):
    frames = blocks[0].shape[0]
    vmem = pl.BlockSpec(memory_space=pltpu.VMEM)
    return pl.pallas_call(
        functools.partial(gather_kernel, n),
        out_shape=jax.ShapeDtypeStruct((frames, C2, CELLS), jnp.bfloat16),
        in_specs=[pl.BlockSpec(memory_space=pltpu.SMEM)] + [vmem] * (HALVES * n),
        out_specs=vmem,
        scratch_shapes=[pltpu.VMEM((frames, CELLS, C2), jnp.bfloat16)],
    )(meta, *blocks)


def exchange(n, blocks):
    return [blocks[0]] + [
        lax.ppermute(blocks[k], "frame", [(i, i ^ k) for i in range(n)]) for k in range(1, n)
    ]


def shards(occ, lengths, w1, w2, tw, wq, wk, wv, wo):
    n = lax.axis_size("frame")
    scenes = lax.axis_size("scene")
    frames = occ.shape[1]
    meta = jnp.stack([lax.axis_index("frame").astype(jnp.int32), lengths[0]])
    maps = conv_maps(n, meta, occ[0], w1, w2)
    moved = [exchange(n, maps[half * n : (half + 1) * n]) for half in range(HALVES)]
    back = []
    partial = jnp.zeros((), jnp.float32)
    for half in range(HALVES):
        out, squares = attend(n, meta, moved[half], tw, wq, wk, wv, wo)
        back += exchange(n, out)
        partial = partial + jnp.sum(squares)
    partial = jnp.broadcast_to(partial, (8, 128))
    step = 1
    while step < n:
        partial = partial + lax.ppermute(partial, "frame", [(i, i ^ step) for i in range(n)])
        step *= 2
    step = 1
    while step < scenes:
        partial = partial + lax.ppermute(partial, "scene", [(i, i ^ step) for i in range(scenes)])
        step *= 2
    encoded = gather(n, meta, back)
    slot_count = float(scenes * n * frames * CELLS * C2)
    return (encoded[None], 0.5 * partial[0, 0] / slot_count)


def solution(mesh):
    placed = (P("scene", "frame", None, None), P("scene"), P(), P(), P(), P(), P(), P(), P())
    return jax.shard_map(
        shards,
        mesh=mesh,
        in_specs=placed,
        out_specs=(P("scene", "frame", None, None), P()),
        check_vma=False,
    )
```

```python
import functools

import jax
import jax.numpy as jnp
from jax import lax
from jax.experimental import pallas as pl
from jax.experimental.pallas import tpu as pltpu
from jax.sharding import PartitionSpec as P


CIN = 64
C1 = 128
C2 = 256
HEADS = 4
HD = 64
HI = 16
ZD = 8
CELLS = 512
ROWS = 8
ROW = 64
HALVES = 2
NORM_EPS = 1e-06
NEG = -1e30
TAIL = 16
VMEM_LIMIT = 24 << 20


def silu(v):
    half = 0.5 * v
    return half + half * jnp.tanh(half)


def shift_z(v, step):
    if step == 0:
        return v
    z = lax.broadcasted_iota(jnp.int32, v.shape, v.ndim - 2)
    moved = pltpu.roll(v, (-step) % ZD, v.ndim - 2)
    keep = (z + step >= 0) & (z + step < ZD)
    return jnp.where(keep, moved, 0.0)


def shift_w(v, step):
    if step == 0:
        return v
    zero = jnp.zeros_like(v[:1])
    if step < 0:
        return jnp.concatenate([zero, v[:-1]], axis=0)
    return jnp.concatenate([v[1:], zero], axis=0)


def store_cols(cols, f, h, v):
    for kz in range(3):
        moved = shift_z(v, kz - 1)
        for kw in range(3):
            lanes = slice((kw * 3 + kz) * C1, (kw * 3 + kz + 1) * C1)
            cols[f, (h + 1) * ROW : (h + 2) * ROW, lanes] = (
                shift_w(moved, kw - 1).reshape(ROW, C1).astype(jnp.bfloat16)
            )


def second_conv(n, far, meta, cols2, w2s, y2, outs):
    frames = cols2.shape[0]
    me = lax.axis_index("frame")
    half = CELLS // 2
    count = CELLS // n
    side = me // (n // 2)
    first = (1 - side if far else side) * half
    acc = jnp.zeros((frames * half, C2), jnp.float32)
    for kh in range(3):
        start = pl.multiple_of(first + kh * ROW, ROW)
        lhs = cols2[:, pl.ds(start, half), :].reshape(frames * half, 9 * C1)
        acc = acc + jnp.dot(lhs, w2s[kh], preferred_element_type=jnp.float32)
    y2[...] = acc
    for f in range(frames):
        valid = jnp.where(me * frames + f < meta[0], 1.0, 0.0)
        for r in range(0, half, ROW):
            rows = slice(f * half + r, f * half + r + ROW)
            y2[rows, :] = silu(y2[rows, :]) * valid
        for k in range(n // 2):
            at = (me ^ (k + n // 2 if far else k)) % (n // 2)
            start = pl.multiple_of(f * half + at * count, count)
            outs[k][f] = y2[pl.ds(start, count), :].astype(jnp.bfloat16)


def conv_kernel(n, meta, occ_hbm, w1_hbm, w2_hbm, *rest):
    outs = rest[: n // 2]
    cols2, w2s = rest[n // 2 : n // 2 + 2]
    occ, w1, w2, t1, t2, w1s, cols1, y1, y2, sems = rest[n // 2 + 2 :]
    frames = occ.shape[0]
    bf16 = jnp.bfloat16

    copies = [pltpu.make_async_copy(w1_hbm, w1, sems.at[0])]
    for f in range(frames):
        copies.append(pltpu.make_async_copy(occ_hbm.at[0, f], occ.at[f], sems.at[1 + f]))
    for half in range(2):
        rows = slice(half * 128, half * 128 + 128)
        copies.append(
            pltpu.make_async_copy(w2_hbm.at[rows, :], w2.at[rows, :], sems.at[1 + frames + half])
        )
    for copy in copies:
        copy.start()
    cols1[:, 0:ROW, :] = jnp.zeros((frames, ROW, cols1.shape[2]), bf16)
    edge = jnp.zeros((frames, ROW, cols2.shape[2]), bf16)
    cols2[:, 0:ROW, :] = edge
    cols2[:, (ROWS + 1) * ROW :, :] = edge
    zero = jnp.zeros((CIN, C1), bf16)

    copies[0].wait()
    t1[...] = w1[...].astype(jnp.float32)
    for kz in range(3):

        def tap1(kh, kw):
            return t1[pl.ds(kh * 9 + kw * 3 + kz, CIN, stride=27), :].astype(bf16)

        for place, (kw, hp) in enumerate([(1, 0), (1, 1), (2, 0), (2, 1), (0, 0), (0, 1)]):
            rows = slice(kz * 384 + place * CIN, kz * 384 + place * CIN + CIN)
            w1s[rows, 0:C1] = tap1(hp + 1, kw)
            w1s[rows, C1 : 2 * C1] = tap1(0, kw) if hp == 1 else zero

    for f in range(frames):
        copies[1 + f].wait()
        for h in range(ROWS):
            upper = occ[f, :, h * 256 : h * 256 + 128]
            lower = occ[f, :, h * 256 + 128 : h * 256 + 256]
            tile = jnp.concatenate([upper, lower], axis=0).astype(jnp.float32).T
            tile = tile.reshape(8, 2, ZD, 128)
            even, odd = tile[:, 0], tile[:, 1]
            for kz in range(3):
                e, o = shift_z(even, kz - 1), shift_z(odd, kz - 1)
                parts = (e, o, shift_w(o, -1))
                for i, part in enumerate(parts):
                    lanes = slice(kz * 384 + i * 128, kz * 384 + i * 128 + 128)
                    cols1[f, (h + 1) * ROW : (h + 2) * ROW, lanes] = part.reshape(ROW, 128).astype(bf16)
        y1[f] = jnp.dot(cols1[f], w1s[...], preferred_element_type=jnp.float32)
        if f == 0:
            copies[1 + frames].wait()
            copies[2 + frames].wait()
        pieces = w2.shape[1] // 128
        for j in range(f * pieces // frames, (f + 1) * pieces // frames):
            for half in range(2):
                t2[half, j * 128 : j * 128 + 128, :] = (
                    w2[half * 128 : half * 128 + 128, j * 128 : j * 128 + 128].astype(jnp.float32).T
                )
        for h in range(ROWS):
            v = (
                y1[f, (h + 1) * ROW : (h + 2) * ROW, 0:C1]
                + y1[f, h * ROW : (h + 1) * ROW, C1 : 2 * C1]
            )
            store_cols(cols2, f, h, silu(v).reshape(8, ZD, C1))
    for kh in range(3):
        for kw in range(3):
            for kz in range(3):
                rows = slice((kw * 3 + kz) * C1, (kw * 3 + kz + 1) * C1)
                for half in range(2):
                    w2s[kh, rows, half * 128 : half * 128 + 128] = t2[
                        half, pl.ds(kh * 9 + kw * 3 + kz, C1, stride=27), :
                    ].astype(bf16)
    second_conv(n, True, meta, cols2, w2s, y2, outs)


def near_kernel(n, meta, cols2, w2s, *rest):
    second_conv(n, False, meta, cols2, w2s, rest[n // 2], rest[: n // 2])


def conv_far(n, meta, occ, w1, w2):
    frames = occ.shape[1]
    count = CELLS // n
    vmem = pl.BlockSpec(memory_space=pltpu.VMEM)
    hbm = pl.BlockSpec(memory_space=pltpu.HBM)
    f32, bf16 = jnp.float32, jnp.bfloat16
    res = pl.pallas_call(
        functools.partial(conv_kernel, n),
        out_shape=[jax.ShapeDtypeStruct((frames, count, C2), bf16)] * (n // 2)
        + [
            jax.ShapeDtypeStruct((frames, (ROWS + 2) * ROW, 9 * C1), bf16),
            jax.ShapeDtypeStruct((3, 9 * C1, C2), bf16),
        ],
        in_specs=[pl.BlockSpec(memory_space=pltpu.SMEM), hbm, hbm, hbm],
        out_specs=[vmem] * (n // 2 + 2),
        scratch_shapes=[
            pltpu.VMEM((frames, CIN, HI * HI * ZD), bf16),
            pltpu.VMEM((CIN * 27, C1), bf16),
            pltpu.VMEM((C2, C1 * 27), bf16),
            pltpu.VMEM((CIN * 27, C1), f32),
            pltpu.VMEM((2, C1 * 27, 128), f32),
            pltpu.VMEM((1152, 2 * C1), bf16),
            pltpu.VMEM((frames, (ROWS + 1) * ROW, 1152), bf16),
            pltpu.VMEM((frames, (ROWS + 1) * ROW, 2 * C1), f32),
            pltpu.VMEM((frames * CELLS // 2, C2), f32),
            pltpu.SemaphoreType.DMA((3 + frames,)),
        ],
        compiler_params=pltpu.CompilerParams(vmem_limit_bytes=40 << 20),
        cost_estimate=pl.CostEstimate(
            flops=2 * frames * CELLS * (C1 * CIN * 27 + C2 * C1 * 27 // 2),
            bytes_accessed=4_000_000,
            transcendentals=frames * CELLS * (C1 + C2),
        ),
    )(meta, *[pltpu.with_memory_space_constraint(x, pltpu.HBM) for x in (occ, w1, w2)])
    return res[: n // 2], res[n // 2], res[n // 2 + 1]


def conv_near(n, meta, cols2, w2s):
    frames = cols2.shape[0]
    count = CELLS // n
    vmem = pl.BlockSpec(memory_space=pltpu.VMEM)
    return pl.pallas_call(
        functools.partial(near_kernel, n),
        out_shape=[jax.ShapeDtypeStruct((frames, count, C2), jnp.bfloat16)] * (n // 2),
        in_specs=[pl.BlockSpec(memory_space=pltpu.SMEM), vmem, vmem],
        out_specs=[vmem] * (n // 2),
        scratch_shapes=[pltpu.VMEM((frames * CELLS // 2, C2), jnp.float32)],
        compiler_params=pltpu.CompilerParams(vmem_limit_bytes=VMEM_LIMIT),
        cost_estimate=pl.CostEstimate(
            flops=2 * frames * CELLS * C2 * C1 * 27 // 2,
            bytes_accessed=4_000_000,
            transcendentals=frames * CELLS * C2 // 2,
        ),
    )(meta, cols2, w2s)


def nt_dot(a, b):
    return lax.dot_general(a, b, (((1,), (1,)), ((), ())), preferred_element_type=jnp.float32)


def attend_kernel(n, half, meta, *rest):
    blocks = rest[:n]
    tw, wq, wk, wv, wo, before = rest[n : n + 6]
    rest = rest[n + 6 :]
    kept, rest = rest[: n // 2 * half], rest[n // 2 * half :]
    outs, squares = rest[:n], rest[n]
    seen, resid, att, bias, ones, p_s, vb = rest[n + 1 :]
    me, length = lax.axis_index("frame"), meta[0]
    frames, count = blocks[0].shape[0], blocks[0].shape[1] // HALVES
    groups = count // 8
    total = n * frames
    rows = total * 8
    bf16 = jnp.bfloat16
    head_of = lax.broadcasted_iota(jnp.int32, (rows, C2), 1) // HD

    edge = jnp.zeros((groups, 1, 8, C2), jnp.float32)
    seen[:, 0:1] = edge
    seen[:, total + 1 : total + 2] = edge
    for k in range(n):
        first = (me ^ k) * frames + 1
        for f in range(frames):
            tile = blocks[k][f, half * count : (half + 1) * count, :].astype(jnp.float32).reshape(groups, 8, C2)
            for g in range(groups):
                seen[g, first + f] = tile[g]

    at = lax.broadcasted_iota(jnp.int32, (rows, rows), 0)
    to = lax.broadcasted_iota(jnp.int32, (rows, rows), 1)
    bias[...] = jnp.where((at % 8 == to % 8) & (to // 8 < length), 0.0, NEG)
    for h in range(HEADS):
        ones[h * rows : (h + 1) * rows, :] = jnp.where(head_of == h, 1.0, 0.0).astype(bf16)
    squares[...] = before[...]

    def group(g, carry):
        slot = g % 2
        mix = jnp.concatenate(
            [seen[g, j : j + total].reshape(rows, C2).astype(bf16) for j in range(3)], axis=1
        )
        summed = jnp.zeros((rows, C2), jnp.float32)
        for j in range(3):
            summed = summed + nt_dot(mix[:, j * C2 : (j + 1) * C2], tw[j])
        here = seen[g, 1 : total + 1].reshape(rows, C2)
        res = (here + silu(summed)).astype(bf16).astype(jnp.float32)
        resid[slot] = res
        mean = jnp.sum(res * res, axis=1, keepdims=True) * (1.0 / C2)
        normed = (res * lax.rsqrt(mean + NORM_EPS)).astype(bf16)
        q = (nt_dot(normed, wq[...]).astype(bf16) * HD ** (-0.5)).astype(bf16)
        keys = nt_dot(normed, wk[...]).astype(bf16)
        values = nt_dot(normed, wv[...]).astype(bf16)
        none = jnp.zeros((rows, C2), bf16)
        for h in range(HEADS):
            mine = head_of == h
            s = nt_dot(q, jnp.where(mine, keys, none)) + bias[...]
            top = jnp.max(s, axis=1, keepdims=True)
            p_s[slot, :, h * rows : (h + 1) * rows] = jnp.exp(s - top).astype(bf16)
            vb[slot, h * rows : (h + 1) * rows, :] = jnp.where(mine, values, none)
        weighted = jnp.dot(p_s[slot], vb[slot], preferred_element_type=jnp.float32)
        sums = jnp.dot(p_s[slot], ones[...], preferred_element_type=jnp.float32)
        attended = (weighted / sums).astype(bf16)
        full = resid[slot] + nt_dot(attended, wo[...])
        t = lax.broadcasted_iota(jnp.int32, (rows, C2), 0) // 8
        full = jnp.where(t < length, full, 0.0).astype(bf16).astype(jnp.float32)
        att[g] = full.reshape(total, 8, C2)
        sq = full * full
        squares[...] = squares[...] + jnp.sum(sq.reshape(total, 8, C2), axis=0)
        return carry

    for g in range(groups):
        group(g, 0)
    for k in range(n):
        first = (me ^ k) * frames
        at = 0
        if half == 1 and k < n // 2:
            outs[k][0 : frames * count, :] = kept[k][...]
            at = frames * count
        for f in range(frames):
            tile = jnp.concatenate([att[g, first + f] for g in range(groups)], axis=0)
            outs[k][at + f * count : at + (f + 1) * count, :] = tile.astype(bf16)
    if half == 1:
        sum_of = jnp.broadcast_to(jnp.sum(squares[...], keepdims=True), (TAIL, C2))
        row = lax.broadcasted_iota(jnp.int32, (TAIL, C2), 0)
        high = sum_of.astype(bf16).astype(jnp.float32)
        middle = (sum_of - high).astype(bf16).astype(jnp.float32)
        low = sum_of - high - middle
        tail = jnp.where(row == 0, high, jnp.where(row == 1, middle, jnp.where(row == 2, low, 0.0)))
        for k in range(n):
            outs[k][outs[k].shape[0] - TAIL :, :] = tail.astype(bf16)


def attend(n, half, meta, blocks, weights, before, kept):
    frames, both, _ = blocks[0].shape
    count = both // HALVES
    total = n * frames
    rows = total * 8
    groups = count // 8
    vmem = pl.BlockSpec(memory_space=pltpu.VMEM)
    sizes = [frames * count] * n
    if half == 1:
        sizes = [frames * (both if k < n // 2 else count) + TAIL for k in range(n)]
    res = pl.pallas_call(
        functools.partial(attend_kernel, n, half),
        out_shape=[jax.ShapeDtypeStruct((size, C2), jnp.bfloat16) for size in sizes]
        + [jax.ShapeDtypeStruct((8, C2), jnp.float32)],
        in_specs=[pl.BlockSpec(memory_space=pltpu.SMEM)] + [vmem] * (n + 6 + len(kept)),
        out_specs=[vmem] * (n + 1),
        scratch_shapes=[
            pltpu.VMEM((groups, total + 2, 8, C2), jnp.float32),
            pltpu.VMEM((2, rows, C2), jnp.float32),
            pltpu.VMEM((groups, total, 8, C2), jnp.float32),
            pltpu.VMEM((rows, rows), jnp.float32),
            pltpu.VMEM((HEADS * rows, C2), jnp.bfloat16),
            pltpu.VMEM((2, rows, HEADS * rows), jnp.bfloat16),
            pltpu.VMEM((2, HEADS * rows, C2), jnp.bfloat16),
        ],
        compiler_params=pltpu.CompilerParams(vmem_limit_bytes=VMEM_LIMIT),
        cost_estimate=pl.CostEstimate(
            flops=2 * groups * rows * C2 * (7 * C2 + 12 * rows),
            bytes_accessed=4_000_000,
            transcendentals=groups * rows * HEADS * rows,
        ),
    )(meta, *blocks, *weights, before, *kept)
    return res[:n], res[n]


def gather_kernel(n, *rest):
    early, late, out, whole = rest[: n // 2], rest[n // 2 : n // 2 + n], rest[-2], rest[-1]
    me = lax.axis_index("frame")
    frames = out.shape[0]
    count = CELLS // n
    part = count // HALVES
    for k in range(n):
        start = pl.multiple_of((me ^ k) * count, count)
        for half in range(HALVES):
            block, first = late[k], 0
            if k >= n // 2 and half == 0:
                block = early[k - n // 2]
            elif k < n // 2:
                first = half * frames * part
            for f in range(frames):
                rows = slice(first + f * part, first + (f + 1) * part)
                whole[f, pl.ds(start + half * part, part), :] = block[rows, :]
    for f in range(frames):
        out[f] = whole[f].astype(jnp.float32).T.astype(jnp.bfloat16)


def gather(n, frames, early, late):
    vmem = pl.BlockSpec(memory_space=pltpu.VMEM)
    return pl.pallas_call(
        functools.partial(gather_kernel, n),
        out_shape=jax.ShapeDtypeStruct((frames, C2, CELLS), jnp.bfloat16),
        in_specs=[vmem] * (len(early) + len(late)),
        out_specs=vmem,
        scratch_shapes=[pltpu.VMEM((frames, CELLS, C2), jnp.bfloat16)],
        compiler_params=pltpu.CompilerParams(vmem_limit_bytes=VMEM_LIMIT),
        cost_estimate=pl.CostEstimate(flops=0, bytes_accessed=4_000_000, transcendentals=0),
    )(*early, *late)


def tally_kernel(n, *rest):
    total = jnp.zeros((TAIL, C2), jnp.float32)
    for k in range(n):
        total = total + rest[k][...].astype(jnp.float32)
    rest[n][...] = jnp.broadcast_to(jnp.sum(total, axis=0, keepdims=True)[:, :128], (8, 128))


def last_tile(rows):
    return pl.BlockSpec((TAIL, C2), lambda i: (rows // TAIL - 1, 0))


def tally(n, blocks):
    return pl.pallas_call(
        functools.partial(tally_kernel, n),
        grid=(1,),
        out_shape=jax.ShapeDtypeStruct((8, 128), jnp.float32),
        in_specs=[last_tile(block.shape[0]) for block in blocks],
        out_specs=pl.BlockSpec((8, 128), lambda i: (0, 0)),
        compiler_params=pltpu.CompilerParams(vmem_limit_bytes=VMEM_LIMIT // 16),
        cost_estimate=pl.CostEstimate(flops=0, bytes_accessed=100_000, transcendentals=0),
    )(*blocks)


def far_of(n):
    return sorted(range(n // 2, n), key=lambda k: (-(k // 2), k))


def near_of(n):
    return sorted(range(1, n // 2), key=lambda k: (-(k // 2), k))


def send(n, k, block):
    return lax.ppermute(block, "frame", [(i, i ^ k) for i in range(n)])


def shards(occ, lengths, w1, w2, tw, wq, wk, wv, wo):
    n = lax.axis_size("frame")
    scenes = lax.axis_size("scene")
    frames = occ.shape[1]
    weights = (tw, wq, wk, wv, wo)
    far, cols2, w2s = conv_far(n, lengths, occ, w1.T, w2)
    moved = [None] * n
    for k in far_of(n):
        moved[k] = send(n, k, far[k - n // 2])
    near = conv_near(n, lengths, cols2, w2s)
    moved[0] = near[0]
    for k in near_of(n):
        moved[k] = send(n, k, near[k])
    squares = jnp.zeros((8, C2), jnp.float32)
    first, squares = attend(n, 0, lengths, moved, weights, squares, [])
    early = {k: send(n, k, first[k]) for k in far_of(n)}
    second, _ = attend(n, 1, lengths, moved, weights, squares, list(first[: n // 2]))
    late = [second[0]] + [None] * (n - 1)
    for k in far_of(n) + near_of(n):
        late[k] = send(n, k, second[k])
    mine = tally(n, late)
    total = mine
    for step in range(1, scenes):
        total = total + lax.ppermute(mine, "scene", [(i, i ^ step) for i in range(scenes)])
    encoded = gather(n, frames, [early[k] for k in range(n // 2, n)], late)
    slot_count = float(scenes * n * frames * CELLS * C2)
    return (encoded[None], 0.5 * total[0, 0] / slot_count)


def solution(mesh):
    placed = (P("scene", "frame", None, None), P("scene"), P(), P(), P(), P(), P(), P(), P())
    return jax.shard_map(
        shards,
        mesh=mesh,
        in_specs=placed,
        out_specs=(P("scene", "frame", None, None), P()),
        check_vma=False,
    )
```

```python
import functools

import jax
import jax.numpy as jnp
from jax import lax
from jax.experimental import pallas as pl
from jax.experimental.pallas import tpu as pltpu
from jax.sharding import PartitionSpec as P


CIN = 64
C1 = 128
C2 = 256
HEADS = 4
HD = 64
HI = 16
ZD = 8
CELLS = 512
ROWS = 8
ROW = 64
HALVES = 2
NORM_EPS = 1e-06
NEG = -1e30
TAIL = 16
VMEM_LIMIT = 24 << 20


def silu(v):
    half = 0.5 * v
    return half + half * jnp.tanh(half)


def shift_z(v, step):
    if step == 0:
        return v
    z = lax.broadcasted_iota(jnp.int32, v.shape, v.ndim - 2)
    moved = pltpu.roll(v, (-step) % ZD, v.ndim - 2)
    keep = (z + step >= 0) & (z + step < ZD)
    return jnp.where(keep, moved, 0.0)


def shift_w(v, step):
    if step == 0:
        return v
    zero = jnp.zeros_like(v[:1])
    if step < 0:
        return jnp.concatenate([zero, v[:-1]], axis=0)
    return jnp.concatenate([v[1:], zero], axis=0)


def store_cols(cols, f, h, v):
    for kz in range(3):
        moved = shift_z(v, kz - 1)
        for kw in range(3):
            lanes = slice((kw * 3 + kz) * C1, (kw * 3 + kz + 1) * C1)
            cols[f, (h + 1) * ROW : (h + 2) * ROW, lanes] = (
                shift_w(moved, kw - 1).reshape(ROW, C1).astype(jnp.bfloat16)
            )


def second_conv(n, far, meta, cols2, w2s, y2, outs):
    frames = cols2.shape[0]
    me = lax.axis_index("frame")
    half = CELLS // 2
    count = CELLS // n
    side = me // (n // 2)
    first = (1 - side if far else side) * half
    acc = jnp.zeros((frames * half, C2), jnp.float32)
    for kh in range(3):
        start = pl.multiple_of(first + kh * ROW, ROW)
        lhs = cols2[:, pl.ds(start, half), :].reshape(frames * half, 9 * C1)
        acc = acc + jnp.dot(lhs, w2s[kh], preferred_element_type=jnp.float32)
    y2[...] = acc
    for f in range(frames):
        valid = jnp.where(me * frames + f < meta[0], 1.0, 0.0)
        for r in range(0, half, ROW):
            rows = slice(f * half + r, f * half + r + ROW)
            y2[rows, :] = silu(y2[rows, :]) * valid
        for k in range(n // 2):
            at = (me ^ (k + n // 2 if far else k)) % (n // 2)
            start = pl.multiple_of(f * half + at * count, count)
            block = y2[pl.ds(start, count), :].astype(jnp.bfloat16)
            if far:
                outs[k][f] = block[: count // 2]
                outs[k + n // 2][f] = block[count // 2 :]
            else:
                outs[k][f] = block


def conv_kernel(n, meta, occ_hbm, w1_hbm, w2_hbm, *rest):
    outs = rest[:n]
    cols2, w2s = rest[n : n + 2]
    occ, w1, w2, t1, t2, w1s, cols1, y1, y2, sems = rest[n + 2 :]
    frames = occ.shape[0]
    bf16 = jnp.bfloat16

    copies = [pltpu.make_async_copy(w1_hbm, w1, sems.at[0])]
    for f in range(frames):
        copies.append(pltpu.make_async_copy(occ_hbm.at[0, f], occ.at[f], sems.at[1 + f]))
    for half in range(2):
        rows = slice(half * 128, half * 128 + 128)
        copies.append(
            pltpu.make_async_copy(w2_hbm.at[rows, :], w2.at[rows, :], sems.at[1 + frames + half])
        )
    for copy in copies:
        copy.start()
    cols1[:, 0:ROW, :] = jnp.zeros((frames, ROW, cols1.shape[2]), bf16)
    edge = jnp.zeros((frames, ROW, cols2.shape[2]), bf16)
    cols2[:, 0:ROW, :] = edge
    cols2[:, (ROWS + 1) * ROW :, :] = edge
    zero = jnp.zeros((CIN, C1), bf16)

    copies[0].wait()
    t1[...] = w1[...].astype(jnp.float32)
    for kz in range(3):

        def tap1(kh, kw):
            return t1[pl.ds(kh * 9 + kw * 3 + kz, CIN, stride=27), :].astype(bf16)

        for place, (kw, hp) in enumerate([(1, 0), (1, 1), (2, 0), (2, 1), (0, 0), (0, 1)]):
            rows = slice(kz * 384 + place * CIN, kz * 384 + place * CIN + CIN)
            w1s[rows, 0:C1] = tap1(hp + 1, kw)
            w1s[rows, C1 : 2 * C1] = tap1(0, kw) if hp == 1 else zero

    for f in range(frames):
        copies[1 + f].wait()
        for h in range(ROWS):
            upper = occ[f, :, h * 256 : h * 256 + 128]
            lower = occ[f, :, h * 256 + 128 : h * 256 + 256]
            tile = jnp.concatenate([upper, lower], axis=0).astype(jnp.float32).T
            tile = tile.reshape(8, 2, ZD, 128)
            even, odd = tile[:, 0], tile[:, 1]
            for kz in range(3):
                e, o = shift_z(even, kz - 1), shift_z(odd, kz - 1)
                parts = (e, o, shift_w(o, -1))
                for i, part in enumerate(parts):
                    lanes = slice(kz * 384 + i * 128, kz * 384 + i * 128 + 128)
                    cols1[f, (h + 1) * ROW : (h + 2) * ROW, lanes] = part.reshape(ROW, 128).astype(bf16)
        y1[f] = jnp.dot(cols1[f], w1s[...], preferred_element_type=jnp.float32)
        if f == 0:
            copies[1 + frames].wait()
            copies[2 + frames].wait()
        pieces = w2.shape[1] // 128
        for j in range(f * pieces // frames, (f + 1) * pieces // frames):
            for half in range(2):
                t2[half, j * 128 : j * 128 + 128, :] = (
                    w2[half * 128 : half * 128 + 128, j * 128 : j * 128 + 128].astype(jnp.float32).T
                )
        for h in range(ROWS):
            v = (
                y1[f, (h + 1) * ROW : (h + 2) * ROW, 0:C1]
                + y1[f, h * ROW : (h + 1) * ROW, C1 : 2 * C1]
            )
            store_cols(cols2, f, h, silu(v).reshape(8, ZD, C1))
    for kh in range(3):
        for kw in range(3):
            for kz in range(3):
                rows = slice((kw * 3 + kz) * C1, (kw * 3 + kz + 1) * C1)
                for half in range(2):
                    w2s[kh, rows, half * 128 : half * 128 + 128] = t2[
                        half, pl.ds(kh * 9 + kw * 3 + kz, C1, stride=27), :
                    ].astype(bf16)
    second_conv(n, True, meta, cols2, w2s, y2, outs)


def near_kernel(n, meta, cols2, w2s, *rest):
    second_conv(n, False, meta, cols2, w2s, rest[n // 2], rest[: n // 2])


def conv_far(n, meta, occ, w1, w2):
    frames = occ.shape[1]
    count = CELLS // n
    vmem = pl.BlockSpec(memory_space=pltpu.VMEM)
    hbm = pl.BlockSpec(memory_space=pltpu.HBM)
    f32, bf16 = jnp.float32, jnp.bfloat16
    res = pl.pallas_call(
        functools.partial(conv_kernel, n),
        out_shape=[jax.ShapeDtypeStruct((frames, count // 2, C2), bf16)] * n
        + [
            jax.ShapeDtypeStruct((frames, (ROWS + 2) * ROW, 9 * C1), bf16),
            jax.ShapeDtypeStruct((3, 9 * C1, C2), bf16),
        ],
        in_specs=[pl.BlockSpec(memory_space=pltpu.SMEM), hbm, hbm, hbm],
        out_specs=[vmem] * (n + 2),
        scratch_shapes=[
            pltpu.VMEM((frames, CIN, HI * HI * ZD), bf16),
            pltpu.VMEM((CIN * 27, C1), bf16),
            pltpu.VMEM((C2, C1 * 27), bf16),
            pltpu.VMEM((CIN * 27, C1), f32),
            pltpu.VMEM((2, C1 * 27, 128), f32),
            pltpu.VMEM((1152, 2 * C1), bf16),
            pltpu.VMEM((frames, (ROWS + 1) * ROW, 1152), bf16),
            pltpu.VMEM((frames, (ROWS + 1) * ROW, 2 * C1), f32),
            pltpu.VMEM((frames * CELLS // 2, C2), f32),
            pltpu.SemaphoreType.DMA((3 + frames,)),
        ],
        compiler_params=pltpu.CompilerParams(vmem_limit_bytes=40 << 20),
        cost_estimate=pl.CostEstimate(
            flops=2 * frames * CELLS * (C1 * CIN * 27 + C2 * C1 * 27 // 2),
            bytes_accessed=4_000_000,
            transcendentals=frames * CELLS * (C1 + C2),
        ),
    )(meta, *[pltpu.with_memory_space_constraint(x, pltpu.HBM) for x in (occ, w1, w2)])
    return res[: n // 2], res[n // 2 : n], res[n], res[n + 1]


def conv_near(n, meta, cols2, w2s):
    frames = cols2.shape[0]
    count = CELLS // n
    vmem = pl.BlockSpec(memory_space=pltpu.VMEM)
    return pl.pallas_call(
        functools.partial(near_kernel, n),
        out_shape=[jax.ShapeDtypeStruct((frames, count, C2), jnp.bfloat16)] * (n // 2),
        in_specs=[pl.BlockSpec(memory_space=pltpu.SMEM), vmem, vmem],
        out_specs=[vmem] * (n // 2),
        scratch_shapes=[pltpu.VMEM((frames * CELLS // 2, C2), jnp.float32)],
        compiler_params=pltpu.CompilerParams(vmem_limit_bytes=VMEM_LIMIT),
        cost_estimate=pl.CostEstimate(
            flops=2 * frames * CELLS * C2 * C1 * 27 // 2,
            bytes_accessed=4_000_000,
            transcendentals=frames * CELLS * C2 // 2,
        ),
    )(meta, cols2, w2s)


def nt_dot(a, b):
    return lax.dot_general(a, b, (((1,), (1,)), ((), ())), preferred_element_type=jnp.float32)


def swap_cells(even, odd):
    upper = lax.broadcasted_iota(jnp.int32, even.shape, even.ndim - 2) < 4
    low = jnp.where(upper, even, pltpu.roll(odd, 4, odd.ndim - 2))
    high = jnp.where(upper, pltpu.roll(even, 4, even.ndim - 2), odd)
    return low, high


def attend_kernel(n, half, meta, *rest):
    blocks = rest[:n]
    tw, wq, wk, wv, wo, before = rest[n : n + 6]
    rest = rest[n + 6 :]
    kept, rest = rest[: n // 2 * half], rest[n // 2 * half :]
    outs, squares = rest[:n], rest[n]
    seen, resid, q_s, k_s, v_s, a_s, kb, vb, p_s, bias, ones = rest[n + 1 :]
    me, length = lax.axis_index("frame"), meta[0]
    frames, count = blocks[0].shape[0], blocks[0].shape[1] // HALVES
    first_cell = [half * count if k < n // 2 else 0 for k in range(n)]
    groups = count // 8
    total = n * frames
    rows = total * 4
    everything = 2 * groups * rows
    f32, bf16 = jnp.float32, jnp.bfloat16
    head_of = lax.broadcasted_iota(jnp.int32, (rows, C2), 1) // HD

    edge = jnp.zeros((groups, 1, 8, C2), f32)
    seen[:, 0:1] = edge
    seen[:, total + 1 : total + 2] = edge
    for k in range(n):
        first = (me ^ k) * frames + 1
        for f in range(frames):
            tile = blocks[k][f, first_cell[k] : first_cell[k] + count, :]
            tile = tile.astype(f32).reshape(groups, 8, C2)
            for g in range(groups):
                seen[g, first + f] = tile[g]

    at = lax.broadcasted_iota(jnp.int32, (rows, rows), 0)
    to = lax.broadcasted_iota(jnp.int32, (rows, rows), 1)
    bias[...] = jnp.where((at % 4 == to % 4) & (to // 4 < length), 0.0, NEG)
    for h in range(HEADS):
        ones[h * rows : (h + 1) * rows, :] = jnp.where(head_of == h, 1.0, 0.0).astype(bf16)

    for g in range(groups):
        summed = jnp.zeros((total * 8, C2), f32)
        for j in range(3):
            mix = seen[g, j : j + total].reshape(total * 8, C2).astype(bf16)
            summed = summed + nt_dot(mix, tw[j])
        res = (seen[g, 1 : total + 1].reshape(total * 8, C2) + silu(summed)).astype(bf16)
        res = res.astype(f32).reshape(total // 2, 2, 8, C2)
        low, high = swap_cells(res[:, 0], res[:, 1])
        for part, value in ((0, low), (1, high)):
            value = value.reshape(rows, C2)
            start = (2 * g + part) * rows
            resid[start : start + rows, :] = value
            mean = jnp.sum(value * value, axis=1, keepdims=True) * (1.0 / C2)
            a_s[start : start + rows, :] = (value * lax.rsqrt(mean + NORM_EPS)).astype(bf16)
    normed = a_s[...]
    q_s[...] = (nt_dot(normed, wq[...]).astype(bf16) * HD ** (-0.5)).astype(bf16)
    k_s[...] = nt_dot(normed, wk[...]).astype(bf16)
    v_s[...] = nt_dot(normed, wv[...]).astype(bf16)

    none = jnp.zeros((rows, C2), bf16)
    for b in range(2 * groups):
        slot = b % 2
        here = slice(b * rows, (b + 1) * rows)
        keys, values = k_s[here, :], v_s[here, :]
        for h in range(HEADS):
            kb[slot, h * rows : (h + 1) * rows, :] = jnp.where(head_of == h, keys, none)
            vb[slot, h * rows : (h + 1) * rows, :] = jnp.where(head_of == h, values, none)
        s = nt_dot(q_s[here, :], kb[slot])
        for h in range(HEADS):
            mine = s[:, h * rows : (h + 1) * rows] + bias[...]
            top = jnp.max(mine, axis=1, keepdims=True)
            p_s[slot, :, h * rows : (h + 1) * rows] = jnp.exp(mine - top).astype(bf16)
        weighted = jnp.dot(p_s[slot], vb[slot], preferred_element_type=f32)
        sums = jnp.dot(p_s[slot], ones[...], preferred_element_type=f32)
        a_s[here, :] = (weighted / sums).astype(bf16)

    full = resid[...] + nt_dot(a_s[...], wo[...])
    t = lax.broadcasted_iota(jnp.int32, (everything, C2), 0) % rows // 4
    full = jnp.where(t < length, full, 0.0).astype(bf16).astype(f32)
    squares[...] = before[...] + jnp.sum((full * full).reshape(everything // 8, 8, C2), axis=0)
    full = full.reshape(groups, 2, total // 2, 8, C2)
    for g in range(groups):
        even, odd = swap_cells(full[g, 0], full[g, 1])
        seen[g, 0:total] = jnp.stack([even, odd], axis=1).reshape(total, 8, C2)

    for k in range(n):
        first = (me ^ k) * frames
        at = 0
        if half == 1 and k < n // 2:
            outs[k][0 : frames * count, :] = kept[k][...]
            at = frames * count
        for f in range(frames):
            tile = jnp.concatenate([seen[g, first + f] for g in range(groups)], axis=0)
            outs[k][at + f * count : at + (f + 1) * count, :] = tile.astype(bf16)
    if half == 1:
        sum_of = jnp.broadcast_to(jnp.sum(squares[...], keepdims=True), (TAIL, C2))
        row = lax.broadcasted_iota(jnp.int32, (TAIL, C2), 0)
        high = sum_of.astype(bf16).astype(f32)
        middle = (sum_of - high).astype(bf16).astype(f32)
        low = sum_of - high - middle
        tail = jnp.where(row == 0, high, jnp.where(row == 1, middle, jnp.where(row == 2, low, 0.0)))
        for k in range(n):
            outs[k][outs[k].shape[0] - TAIL :, :] = tail.astype(bf16)


def attend(n, half, meta, blocks, weights, before, kept):
    frames, both, _ = blocks[0].shape
    count = both // HALVES
    total = n * frames
    rows = total * 4
    groups = count // 8
    everything = 2 * groups * rows
    vmem = pl.BlockSpec(memory_space=pltpu.VMEM)
    f32, bf16 = jnp.float32, jnp.bfloat16
    sizes = [frames * count] * n
    if half == 1:
        sizes = [frames * (both if k < n // 2 else count) + TAIL for k in range(n)]
    res = pl.pallas_call(
        functools.partial(attend_kernel, n, half),
        out_shape=[jax.ShapeDtypeStruct((size, C2), bf16) for size in sizes]
        + [jax.ShapeDtypeStruct((8, C2), f32)],
        in_specs=[pl.BlockSpec(memory_space=pltpu.SMEM)] + [vmem] * (n + 6 + len(kept)),
        out_specs=[vmem] * (n + 1),
        scratch_shapes=[
            pltpu.VMEM((groups, total + 2, 8, C2), f32),
            pltpu.VMEM((everything, C2), f32),
            pltpu.VMEM((everything, C2), bf16),
            pltpu.VMEM((everything, C2), bf16),
            pltpu.VMEM((everything, C2), bf16),
            pltpu.VMEM((everything, C2), bf16),
            pltpu.VMEM((2, HEADS * rows, C2), bf16),
            pltpu.VMEM((2, HEADS * rows, C2), bf16),
            pltpu.VMEM((2, rows, HEADS * rows), bf16),
            pltpu.VMEM((rows, rows), f32),
            pltpu.VMEM((HEADS * rows, C2), bf16),
        ],
        compiler_params=pltpu.CompilerParams(vmem_limit_bytes=VMEM_LIMIT),
        cost_estimate=pl.CostEstimate(
            flops=2 * everything * C2 * (7 * C2 + 12 * rows),
            bytes_accessed=4_000_000,
            transcendentals=everything * HEADS * rows,
        ),
    )(meta, *blocks, *weights, before, *kept)
    return res[:n], res[n]


def gather_kernel(n, *rest):
    early, late, out, whole = rest[: n // 2], rest[n // 2 : n // 2 + n], rest[-2], rest[-1]
    me = lax.axis_index("frame")
    frames = out.shape[0]
    count = CELLS // n
    part = count // HALVES
    for k in range(n):
        start = pl.multiple_of((me ^ k) * count, count)
        for half in range(HALVES):
            block, first = late[k], 0
            if k >= n // 2 and half == 0:
                block = early[k - n // 2]
            elif k < n // 2:
                first = half * frames * part
            for f in range(frames):
                rows = slice(first + f * part, first + (f + 1) * part)
                whole[f, pl.ds(start + half * part, part), :] = block[rows, :]
    for f in range(frames):
        out[f] = whole[f].astype(jnp.float32).T.astype(jnp.bfloat16)


def gather(n, frames, early, late):
    vmem = pl.BlockSpec(memory_space=pltpu.VMEM)
    return pl.pallas_call(
        functools.partial(gather_kernel, n),
        out_shape=jax.ShapeDtypeStruct((frames, C2, CELLS), jnp.bfloat16),
        in_specs=[vmem] * (len(early) + len(late)),
        out_specs=vmem,
        scratch_shapes=[pltpu.VMEM((frames, CELLS, C2), jnp.bfloat16)],
        compiler_params=pltpu.CompilerParams(vmem_limit_bytes=VMEM_LIMIT),
        cost_estimate=pl.CostEstimate(flops=0, bytes_accessed=4_000_000, transcendentals=0),
    )(*early, *late)


def tally_kernel(n, *rest):
    total = jnp.zeros((TAIL, C2), jnp.float32)
    for k in range(n):
        total = total + rest[k][...].astype(jnp.float32)
    rest[n][...] = jnp.broadcast_to(jnp.sum(total, axis=0, keepdims=True)[:, :128], (8, 128))


def last_tile(rows):
    return pl.BlockSpec((TAIL, C2), lambda i: (rows // TAIL - 1, 0))


def tally(n, blocks):
    return pl.pallas_call(
        functools.partial(tally_kernel, n),
        grid=(1,),
        out_shape=jax.ShapeDtypeStruct((8, 128), jnp.float32),
        in_specs=[last_tile(block.shape[0]) for block in blocks],
        out_specs=pl.BlockSpec((8, 128), lambda i: (0, 0)),
        compiler_params=pltpu.CompilerParams(vmem_limit_bytes=VMEM_LIMIT // 16),
        cost_estimate=pl.CostEstimate(flops=0, bytes_accessed=100_000, transcendentals=0),
    )(*blocks)


def finish_kernel(scale, mine, *rest):
    total = mine[...]
    for other in rest[:-1]:
        total = total + other[...]
    rest[-1][0, 0] = jnp.max(total) * scale


def finish(scale, mine, others):
    vmem = pl.BlockSpec(memory_space=pltpu.VMEM)
    return pl.pallas_call(
        functools.partial(finish_kernel, scale),
        out_shape=jax.ShapeDtypeStruct((1, 1), jnp.float32),
        in_specs=[vmem] * (1 + len(others)),
        out_specs=pl.BlockSpec(memory_space=pltpu.SMEM),
        compiler_params=pltpu.CompilerParams(vmem_limit_bytes=VMEM_LIMIT // 16),
        cost_estimate=pl.CostEstimate(flops=0, bytes_accessed=100_000, transcendentals=0),
    )(mine, *others)


def far_of(n):
    return list(range(n // 2, n))


def near_of(n):
    return list(range(1, n // 2))


def send(n, k, block):
    return lax.ppermute(block, "frame", [(i, i ^ k) for i in range(n)])


def shards(occ, lengths, w1, w2, tw, wq, wk, wv, wo):
    n = lax.axis_size("frame")
    scenes = lax.axis_size("scene")
    frames = occ.shape[1]
    weights = (tw, wq, wk, wv, wo)
    far0, far1, cols2, w2s = conv_far(n, lengths, occ, w1.T, w2)
    moved0, moved1 = [None] * n, [None] * n
    for k in far_of(n):
        moved0[k] = send(n, k, far0[k - n // 2])
    near = conv_near(n, lengths, cols2, w2s)
    moved0[0] = moved1[0] = near[0]
    for k in near_of(n):
        moved0[k] = moved1[k] = send(n, k, near[k])
    for k in far_of(n):
        moved1[k] = send(n, k, far1[k - n // 2])
    squares = jnp.zeros((8, C2), jnp.float32)
    first, squares = attend(n, 0, lengths, moved0, weights, squares, [])
    early = {k: send(n, k, first[k]) for k in far_of(n)}
    second, _ = attend(n, 1, lengths, moved1, weights, squares, list(first[: n // 2]))
    late = [second[0]] + [None] * (n - 1)
    for k in far_of(n) + near_of(n):
        late[k] = send(n, k, second[k])
    mine = tally(n, late)
    others = []
    for step in range(1, scenes):
        others.append(lax.ppermute(mine, "scene", [(i, i ^ step) for i in range(scenes)]))
    encoded = gather(n, frames, [early[k] for k in range(n // 2, n)], late)
    scale = 0.5 / float(scenes * n * frames * CELLS * C2)
    loss = finish(scale, mine, others)
    return (encoded[None], loss.reshape(()))


def solution(mesh):
    placed = (P("scene", "frame", None, None), P("scene"), P(), P(), P(), P(), P(), P(), P())
    return jax.shard_map(
        shards,
        mesh=mesh,
        in_specs=placed,
        out_specs=(P("scene", "frame", None, None), P()),
        check_vma=False,
    )
```

```python
import functools

import jax
import jax.numpy as jnp
from jax import lax
from jax.experimental import pallas as pl
from jax.experimental.pallas import tpu as pltpu
from jax.sharding import PartitionSpec as P


CIN = 64
C1 = 128
C2 = 256
HEADS = 4
HD = 64
HI = 16
ZD = 8
CELLS = 512
ROWS = 8
ROW = 64
HALVES = 2
NORM_EPS = 1e-06
NEG = -1e30
TAIL = 16
VMEM_LIMIT = 24 << 20


def silu(v):
    half = 0.5 * v
    return half + half * jnp.tanh(half)


def shift_z(v, step):
    if step == 0:
        return v
    z = lax.broadcasted_iota(jnp.int32, v.shape, v.ndim - 2)
    moved = pltpu.roll(v, (-step) % ZD, v.ndim - 2)
    keep = (z + step >= 0) & (z + step < ZD)
    return jnp.where(keep, moved, 0.0)


def shift_w(v, step):
    if step == 0:
        return v
    zero = jnp.zeros_like(v[:1])
    if step < 0:
        return jnp.concatenate([zero, v[:-1]], axis=0)
    return jnp.concatenate([v[1:], zero], axis=0)


def store_cols(cols, f, h, v):
    for kz in range(3):
        moved = shift_z(v, kz - 1)
        for kw in range(3):
            lanes = slice((kw * 3 + kz) * C1, (kw * 3 + kz + 1) * C1)
            cols[f, (h + 1) * ROW : (h + 2) * ROW, lanes] = (
                shift_w(moved, kw - 1).reshape(ROW, C1).astype(jnp.bfloat16)
            )


def second_conv(n, far, meta, cols2, w2s, y2, outs):
    frames = cols2.shape[0]
    me = lax.axis_index("frame")
    half = CELLS // 2
    count = CELLS // n
    side = me // (n // 2)
    first = (1 - side if far else side) * half
    acc = jnp.zeros((frames * half, C2), jnp.float32)
    for kh in range(3):
        start = pl.multiple_of(first + kh * ROW, ROW)
        lhs = cols2[:, pl.ds(start, half), :].reshape(frames * half, 9 * C1)
        acc = acc + jnp.dot(lhs, w2s[kh], preferred_element_type=jnp.float32)
    y2[...] = acc
    for f in range(frames):
        valid = jnp.where(me * frames + f < meta[0], 1.0, 0.0)
        for r in range(0, half, ROW):
            rows = slice(f * half + r, f * half + r + ROW)
            y2[rows, :] = silu(y2[rows, :]) * valid
        for k in range(n // 2):
            at = (me ^ (k + n // 2 if far else k)) % (n // 2)
            start = pl.multiple_of(f * half + at * count, count)
            block = y2[pl.ds(start, count), :].astype(jnp.bfloat16)
            if far:
                outs[k][f] = block[: count // 2]
                outs[k + n // 2][f] = block[count // 2 :]
            else:
                outs[k][f] = block


def conv_kernel(n, meta, occ_hbm, w1_hbm, w2_hbm, *rest):
    outs = rest[:n]
    cols2, w2s = rest[n : n + 2]
    occ, w1, w2, t1, t2, w1s, cols1, y1, y2, sems = rest[n + 2 :]
    frames = occ.shape[0]
    bf16 = jnp.bfloat16

    copies = [pltpu.make_async_copy(w1_hbm, w1, sems.at[0])]
    for f in range(frames):
        copies.append(pltpu.make_async_copy(occ_hbm.at[0, f], occ.at[f], sems.at[1 + f]))
    for half in range(2):
        rows = slice(half * 128, half * 128 + 128)
        copies.append(
            pltpu.make_async_copy(w2_hbm.at[rows, :], w2.at[rows, :], sems.at[1 + frames + half])
        )
    for copy in copies:
        copy.start()
    cols1[:, 0:ROW, :] = jnp.zeros((frames, ROW, cols1.shape[2]), bf16)
    edge = jnp.zeros((frames, ROW, cols2.shape[2]), bf16)
    cols2[:, 0:ROW, :] = edge
    cols2[:, (ROWS + 1) * ROW :, :] = edge
    zero = jnp.zeros((CIN, C1), bf16)

    copies[0].wait()
    t1[...] = w1[...].astype(jnp.float32)
    for kz in range(3):

        def tap1(kh, kw):
            return t1[pl.ds(kh * 9 + kw * 3 + kz, CIN, stride=27), :].astype(bf16)

        for place, (kw, hp) in enumerate([(1, 0), (1, 1), (2, 0), (2, 1), (0, 0), (0, 1)]):
            rows = slice(kz * 384 + place * CIN, kz * 384 + place * CIN + CIN)
            w1s[rows, 0:C1] = tap1(hp + 1, kw)
            w1s[rows, C1 : 2 * C1] = tap1(0, kw) if hp == 1 else zero

    for f in range(frames):
        copies[1 + f].wait()
        for h in range(ROWS):
            upper = occ[f, :, h * 256 : h * 256 + 128]
            lower = occ[f, :, h * 256 + 128 : h * 256 + 256]
            tile = jnp.concatenate([upper, lower], axis=0).astype(jnp.float32).T
            tile = tile.reshape(8, 2, ZD, 128)
            even, odd = tile[:, 0], tile[:, 1]
            for kz in range(3):
                e, o = shift_z(even, kz - 1), shift_z(odd, kz - 1)
                parts = (e, o, shift_w(o, -1))
                for i, part in enumerate(parts):
                    lanes = slice(kz * 384 + i * 128, kz * 384 + i * 128 + 128)
                    cols1[f, (h + 1) * ROW : (h + 2) * ROW, lanes] = part.reshape(ROW, 128).astype(bf16)
        y1[f] = jnp.dot(cols1[f], w1s[...], preferred_element_type=jnp.float32)
        if f == 0:
            copies[1 + frames].wait()
            copies[2 + frames].wait()
        pieces = w2.shape[1] // 128
        for j in range(f * pieces // frames, (f + 1) * pieces // frames):
            for half in range(2):
                t2[half, j * 128 : j * 128 + 128, :] = (
                    w2[half * 128 : half * 128 + 128, j * 128 : j * 128 + 128].astype(jnp.float32).T
                )
        for h in range(ROWS):
            v = (
                y1[f, (h + 1) * ROW : (h + 2) * ROW, 0:C1]
                + y1[f, h * ROW : (h + 1) * ROW, C1 : 2 * C1]
            )
            store_cols(cols2, f, h, silu(v).reshape(8, ZD, C1))
    for kh in range(3):
        for kw in range(3):
            for kz in range(3):
                rows = slice((kw * 3 + kz) * C1, (kw * 3 + kz + 1) * C1)
                for half in range(2):
                    w2s[kh, rows, half * 128 : half * 128 + 128] = t2[
                        half, pl.ds(kh * 9 + kw * 3 + kz, C1, stride=27), :
                    ].astype(bf16)
    second_conv(n, True, meta, cols2, w2s, y2, outs)


def near_kernel(n, meta, cols2, w2s, *rest):
    second_conv(n, False, meta, cols2, w2s, rest[n // 2], rest[: n // 2])


def conv_far(n, meta, occ, w1, w2):
    frames = occ.shape[1]
    count = CELLS // n
    vmem = pl.BlockSpec(memory_space=pltpu.VMEM)
    hbm = pl.BlockSpec(memory_space=pltpu.HBM)
    f32, bf16 = jnp.float32, jnp.bfloat16
    res = pl.pallas_call(
        functools.partial(conv_kernel, n),
        out_shape=[jax.ShapeDtypeStruct((frames, count // 2, C2), bf16)] * n
        + [
            jax.ShapeDtypeStruct((frames, (ROWS + 2) * ROW, 9 * C1), bf16),
            jax.ShapeDtypeStruct((3, 9 * C1, C2), bf16),
        ],
        in_specs=[pl.BlockSpec(memory_space=pltpu.SMEM), hbm, hbm, hbm],
        out_specs=[vmem] * (n + 2),
        scratch_shapes=[
            pltpu.VMEM((frames, CIN, HI * HI * ZD), bf16),
            pltpu.VMEM((CIN * 27, C1), bf16),
            pltpu.VMEM((C2, C1 * 27), bf16),
            pltpu.VMEM((CIN * 27, C1), f32),
            pltpu.VMEM((2, C1 * 27, 128), f32),
            pltpu.VMEM((1152, 2 * C1), bf16),
            pltpu.VMEM((frames, (ROWS + 1) * ROW, 1152), bf16),
            pltpu.VMEM((frames, (ROWS + 1) * ROW, 2 * C1), f32),
            pltpu.VMEM((frames * CELLS // 2, C2), f32),
            pltpu.SemaphoreType.DMA((3 + frames,)),
        ],
        compiler_params=pltpu.CompilerParams(vmem_limit_bytes=40 << 20),
        cost_estimate=pl.CostEstimate(
            flops=2 * frames * CELLS * (C1 * CIN * 27 + C2 * C1 * 27 // 2),
            bytes_accessed=4_000_000,
            transcendentals=frames * CELLS * (C1 + C2),
        ),
    )(meta, *[pltpu.with_memory_space_constraint(x, pltpu.HBM) for x in (occ, w1, w2)])
    return res[: n // 2], res[n // 2 : n], res[n], res[n + 1]


def conv_near(n, meta, cols2, w2s):
    frames = cols2.shape[0]
    count = CELLS // n
    vmem = pl.BlockSpec(memory_space=pltpu.VMEM)
    return pl.pallas_call(
        functools.partial(near_kernel, n),
        out_shape=[jax.ShapeDtypeStruct((frames, count, C2), jnp.bfloat16)] * (n // 2),
        in_specs=[pl.BlockSpec(memory_space=pltpu.SMEM), vmem, vmem],
        out_specs=[vmem] * (n // 2),
        scratch_shapes=[pltpu.VMEM((frames * CELLS // 2, C2), jnp.float32)],
        compiler_params=pltpu.CompilerParams(vmem_limit_bytes=VMEM_LIMIT),
        cost_estimate=pl.CostEstimate(
            flops=2 * frames * CELLS * C2 * C1 * 27 // 2,
            bytes_accessed=4_000_000,
            transcendentals=frames * CELLS * C2 // 2,
        ),
    )(meta, cols2, w2s)


def nt_dot(a, b):
    return lax.dot_general(a, b, (((1,), (1,)), ((), ())), preferred_element_type=jnp.float32)


def swap_cells(even, odd):
    upper = lax.broadcasted_iota(jnp.int32, even.shape, even.ndim - 2) < 4
    low = jnp.where(upper, even, pltpu.roll(odd, 4, odd.ndim - 2))
    high = jnp.where(upper, pltpu.roll(even, 4, even.ndim - 2), odd)
    return low, high


def attend_kernel(n, half, meta, *rest):
    blocks = rest[:n]
    tw, wq, wk, wv, wo, before = rest[n : n + 6]
    rest = rest[n + 6 :]
    kept, rest = rest[: n // 2 * half], rest[n // 2 * half :]
    outs, squares = rest[:n], rest[n]
    seen, resid, q_s, k_s, v_s, a_s, kb, vb, p_s, bias, s_s, ones = rest[n + 1 :]
    me, length = lax.axis_index("frame"), meta[0]
    frames, count = blocks[0].shape[0], blocks[0].shape[1] // HALVES
    first_cell = [half * count if k < n // 2 else 0 for k in range(n)]
    groups = count // 8
    total = n * frames
    rows = total * 4
    f32, bf16 = jnp.float32, jnp.bfloat16
    head_of = lax.broadcasted_iota(jnp.int32, (rows, C2), 1) // HD

    edge = jnp.zeros((groups, 1, 8, C2), f32)
    seen[:, 0:1] = edge
    seen[:, total + 1 : total + 2] = edge
    for k in range(n):
        first = (me ^ k) * frames + 1
        for f in range(frames):
            tile = blocks[k][f, first_cell[k] : first_cell[k] + count, :]
            tile = tile.astype(f32).reshape(groups, 8, C2)
            for g in range(groups):
                seen[g, first + f] = tile[g]

    at = lax.broadcasted_iota(jnp.int32, (rows, rows), 0)
    to = lax.broadcasted_iota(jnp.int32, (rows, rows), 1)
    bias[...] = jnp.where((at & 3 == to & 3) & (to >> 2 < length), 0.0, NEG)
    for h in range(HEADS):
        ones[h * rows : (h + 1) * rows, :] = jnp.where(head_of == h, 1.0, 0.0).astype(bf16)
    valid = lax.broadcasted_iota(jnp.int32, (rows, C2), 0) >> 2 < length
    none = jnp.zeros((rows, C2), bf16)

    def project(g):
        summed = jnp.zeros((total * 8, C2), f32)
        for j in range(3):
            mix = seen[g, j : j + total].reshape(total * 8, C2).astype(bf16)
            summed = summed + nt_dot(mix, tw[j])
        res = (seen[g, 1 : total + 1].reshape(total * 8, C2) + silu(summed)).astype(bf16)
        res = res.astype(f32).reshape(total // 2, 2, 8, C2)
        for part, value in enumerate(swap_cells(res[:, 0], res[:, 1])):
            value = value.reshape(rows, C2)
            start = (2 * g + part) * rows
            resid[start : start + rows, :] = value
            mean = jnp.sum(value * value, axis=1, keepdims=True) * (1.0 / C2)
            a_s[start : start + rows, :] = (value * lax.rsqrt(mean + NORM_EPS)).astype(bf16)

    def qkv(start, size):
        some = slice(start, start + size)
        q_s[some, :] = (nt_dot(a_s[some, :], wq[...]).astype(bf16) * HD ** (-0.5)).astype(bf16)
        k_s[some, :] = nt_dot(a_s[some, :], wk[...]).astype(bf16)
        v_s[some, :] = nt_dot(a_s[some, :], wv[...]).astype(bf16)

    def score(b):
        here = slice(b * rows, (b + 1) * rows)
        keys, values = k_s[here, :], v_s[here, :]
        for h in range(HEADS):
            kb[b % 3, h * rows : (h + 1) * rows, :] = jnp.where(head_of == h, keys, none)
            vb[b % 3, h * rows : (h + 1) * rows, :] = jnp.where(head_of == h, values, none)
        s_s[b % 3] = nt_dot(q_s[here, :], kb[b % 3])

    def soften(b):
        for h in range(HEADS):
            mine = s_s[b % 3, :, h * rows : (h + 1) * rows] + bias[...]
            top = jnp.max(mine, axis=1, keepdims=True)
            p_s[b % 3, :, h * rows : (h + 1) * rows] = jnp.exp(mine - top).astype(bf16)

    def weigh(b):
        here = slice(b * rows, (b + 1) * rows)
        weighted = jnp.dot(p_s[b % 3], vb[b % 3], preferred_element_type=f32)
        sums = jnp.dot(p_s[b % 3], ones[...], preferred_element_type=f32)
        a_s[here, :] = (weighted / sums).astype(bf16)

    def emit(g):
        parts = []
        add = jnp.zeros((8, C2), f32)
        for part in range(2):
            here = slice((2 * g + part) * rows, (2 * g + part + 1) * rows)
            full = resid[here, :] + nt_dot(a_s[here, :], wo[...])
            full = jnp.where(valid, full, 0.0).astype(bf16).astype(f32)
            add = add + jnp.sum((full * full).reshape(rows // 8, 8, C2), axis=0)
            parts.append(full.reshape(total // 2, 8, C2))
        squares[...] = squares[...] + add
        even, odd = swap_cells(*parts)
        seen[g, 0:total] = jnp.stack([even, odd], axis=1).reshape(total, 8, C2)

    squares[...] = before[...]
    last = 2 * groups - 1
    for g in range(groups):
        project(g)
    for b in range(0, 2 * groups, 4):
        qkv(b * rows, min(4, 2 * groups - b) * rows)
    score(0)
    for b in range(2 * groups):
        if b < last:
            score(b + 1)
        soften(b)
        if b > 0:
            weigh(b - 1)
        if b > 1 and b % 2 == 0:
            emit(b // 2 - 1)
    weigh(last)
    emit(groups - 1)

    for k in range(n):
        first = (me ^ k) * frames
        at = 0
        if half == 1 and k < n // 2:
            outs[k][0 : frames * count, :] = kept[k][...]
            at = frames * count
        for f in range(frames):
            tile = jnp.concatenate([seen[g, first + f] for g in range(groups)], axis=0)
            outs[k][at + f * count : at + (f + 1) * count, :] = tile.astype(bf16)
    if half == 1:
        sum_of = jnp.broadcast_to(jnp.sum(squares[...], keepdims=True), (TAIL, C2))
        row = lax.broadcasted_iota(jnp.int32, (TAIL, C2), 0)
        high = sum_of.astype(bf16).astype(f32)
        middle = (sum_of - high).astype(bf16).astype(f32)
        low = sum_of - high - middle
        tail = jnp.where(row == 0, high, jnp.where(row == 1, middle, jnp.where(row == 2, low, 0.0)))
        for k in range(n):
            outs[k][outs[k].shape[0] - TAIL :, :] = tail.astype(bf16)


def attend(n, half, meta, blocks, weights, before, kept):
    frames, both, _ = blocks[0].shape
    count = both // HALVES
    total = n * frames
    rows = total * 4
    groups = count // 8
    everything = 2 * groups * rows
    vmem = pl.BlockSpec(memory_space=pltpu.VMEM)
    f32, bf16 = jnp.float32, jnp.bfloat16
    sizes = [frames * count] * n
    if half == 1:
        sizes = [frames * (both if k < n // 2 else count) + TAIL for k in range(n)]
    res = pl.pallas_call(
        functools.partial(attend_kernel, n, half),
        out_shape=[jax.ShapeDtypeStruct((size, C2), bf16) for size in sizes]
        + [jax.ShapeDtypeStruct((8, C2), f32)],
        in_specs=[pl.BlockSpec(memory_space=pltpu.SMEM)] + [vmem] * (n + 6 + len(kept)),
        out_specs=[vmem] * (n + 1),
        scratch_shapes=[
            pltpu.VMEM((groups, total + 2, 8, C2), f32),
            pltpu.VMEM((everything, C2), f32),
            pltpu.VMEM((everything, C2), bf16),
            pltpu.VMEM((everything, C2), bf16),
            pltpu.VMEM((everything, C2), bf16),
            pltpu.VMEM((everything, C2), bf16),
            pltpu.VMEM((3, HEADS * rows, C2), bf16),
            pltpu.VMEM((3, HEADS * rows, C2), bf16),
            pltpu.VMEM((3, rows, HEADS * rows), bf16),
            pltpu.VMEM((rows, rows), f32),
            pltpu.VMEM((3, rows, HEADS * rows), f32),
            pltpu.VMEM((HEADS * rows, C2), bf16),
        ],
        compiler_params=pltpu.CompilerParams(vmem_limit_bytes=VMEM_LIMIT),
        cost_estimate=pl.CostEstimate(
            flops=2 * everything * C2 * (7 * C2 + 12 * rows),
            bytes_accessed=4_000_000,
            transcendentals=everything * HEADS * rows,
        ),
    )(meta, *blocks, *weights, before, *kept)
    return res[:n], res[n]


def gather_kernel(n, *rest):
    early, late, out, whole = rest[: n // 2], rest[n // 2 : n // 2 + n], rest[-2], rest[-1]
    me = lax.axis_index("frame")
    frames = out.shape[0]
    count = CELLS // n
    part = count // HALVES
    for k in range(n):
        start = pl.multiple_of((me ^ k) * count, count)
        for half in range(HALVES):
            block, first = late[k], 0
            if k >= n // 2 and half == 0:
                block = early[k - n // 2]
            elif k < n // 2:
                first = half * frames * part
            for f in range(frames):
                rows = slice(first + f * part, first + (f + 1) * part)
                whole[f, pl.ds(start + half * part, part), :] = block[rows, :]
    for f in range(frames):
        out[f] = whole[f].astype(jnp.float32).T.astype(jnp.bfloat16)


def gather(n, frames, early, late):
    vmem = pl.BlockSpec(memory_space=pltpu.VMEM)
    return pl.pallas_call(
        functools.partial(gather_kernel, n),
        out_shape=jax.ShapeDtypeStruct((frames, C2, CELLS), jnp.bfloat16),
        in_specs=[vmem] * (len(early) + len(late)),
        out_specs=vmem,
        scratch_shapes=[pltpu.VMEM((frames, CELLS, C2), jnp.bfloat16)],
        compiler_params=pltpu.CompilerParams(vmem_limit_bytes=VMEM_LIMIT),
        cost_estimate=pl.CostEstimate(flops=0, bytes_accessed=4_000_000, transcendentals=0),
    )(*early, *late)


def tally_kernel(n, *rest):
    total = jnp.zeros((TAIL, C2), jnp.float32)
    for k in range(n):
        total = total + rest[k][...].astype(jnp.float32)
    rest[n][...] = jnp.broadcast_to(jnp.sum(total, axis=0, keepdims=True)[:, :128], (8, 128))


def last_tile(rows):
    return pl.BlockSpec((TAIL, C2), lambda i: (rows // TAIL - 1, 0))


def tally(n, blocks):
    return pl.pallas_call(
        functools.partial(tally_kernel, n),
        grid=(1,),
        out_shape=jax.ShapeDtypeStruct((8, 128), jnp.float32),
        in_specs=[last_tile(block.shape[0]) for block in blocks],
        out_specs=pl.BlockSpec((8, 128), lambda i: (0, 0)),
        compiler_params=pltpu.CompilerParams(vmem_limit_bytes=VMEM_LIMIT // 16),
        cost_estimate=pl.CostEstimate(flops=0, bytes_accessed=100_000, transcendentals=0),
    )(*blocks)


def finish_kernel(scale, mine, *rest):
    total = mine[...]
    for other in rest[:-1]:
        total = total + other[...]
    rest[-1][0, 0] = jnp.max(total) * scale


def finish(scale, mine, others):
    vmem = pl.BlockSpec(memory_space=pltpu.VMEM)
    return pl.pallas_call(
        functools.partial(finish_kernel, scale),
        out_shape=jax.ShapeDtypeStruct((1, 1), jnp.float32),
        in_specs=[vmem] * (1 + len(others)),
        out_specs=pl.BlockSpec(memory_space=pltpu.SMEM),
        compiler_params=pltpu.CompilerParams(vmem_limit_bytes=VMEM_LIMIT // 16),
        cost_estimate=pl.CostEstimate(flops=0, bytes_accessed=100_000, transcendentals=0),
    )(mine, *others)


def far_of(n):
    return list(range(n // 2, n))


def near_of(n):
    return list(range(1, n // 2))


def send(n, k, block):
    return lax.ppermute(block, "frame", [(i, i ^ k) for i in range(n)])


def shards(occ, lengths, w1, w2, tw, wq, wk, wv, wo):
    n = lax.axis_size("frame")
    scenes = lax.axis_size("scene")
    frames = occ.shape[1]
    weights = (tw, wq, wk, wv, wo)
    far0, far1, cols2, w2s = conv_far(n, lengths, occ, w1.T, w2)
    moved0, moved1 = [None] * n, [None] * n
    for k in far_of(n):
        moved0[k] = send(n, k, far0[k - n // 2])
    near = conv_near(n, lengths, cols2, w2s)
    moved0[0] = moved1[0] = near[0]
    for k in near_of(n):
        moved0[k] = moved1[k] = send(n, k, near[k])
    for k in far_of(n):
        moved1[k] = send(n, k, far1[k - n // 2])
    squares = jnp.zeros((8, C2), jnp.float32)
    first, squares = attend(n, 0, lengths, moved0, weights, squares, [])
    early = {k: send(n, k, first[k]) for k in far_of(n)}
    second, _ = attend(n, 1, lengths, moved1, weights, squares, list(first[: n // 2]))
    late = [second[0]] + [None] * (n - 1)
    for k in far_of(n) + near_of(n):
        late[k] = send(n, k, second[k])
    mine = tally(n, late)
    others = []
    for step in range(1, scenes):
        others.append(lax.ppermute(mine, "scene", [(i, i ^ step) for i in range(scenes)]))
    encoded = gather(n, frames, [early[k] for k in range(n // 2, n)], late)
    scale = 0.5 / float(scenes * n * frames * CELLS * C2)
    loss = finish(scale, mine, others)
    return (encoded[None], loss.reshape(()))


def solution(mesh):
    placed = (P("scene", "frame", None, None), P("scene"), P(), P(), P(), P(), P(), P(), P())
    return jax.shard_map(
        shards,
        mesh=mesh,
        in_specs=placed,
        out_specs=(P("scene", "frame", None, None), P()),
        check_vma=False,
    )
```

```python
import functools

import jax
import jax.numpy as jnp
from jax import lax
from jax.experimental import pallas as pl
from jax.experimental.pallas import tpu as pltpu
from jax.sharding import PartitionSpec as P


CIN = 64
C1 = 128
C2 = 256
HEADS = 4
HD = 64
HI = 16
ZD = 8
CELLS = 512
ROWS = 8
ROW = 64
HALVES = 2
NORM_EPS = 1e-06
NEG = -1e30
TAIL = 16
VMEM_LIMIT = 24 << 20


def silu(v):
    half = 0.5 * v
    return half + half * jnp.tanh(half)


def shift_z(v, step):
    if step == 0:
        return v
    z = lax.broadcasted_iota(jnp.int32, v.shape, v.ndim - 2)
    moved = pltpu.roll(v, (-step) % ZD, v.ndim - 2)
    keep = (z + step >= 0) & (z + step < ZD)
    return jnp.where(keep, moved, 0.0)


def shift_w(v, step):
    if step == 0:
        return v
    zero = jnp.zeros_like(v[:1])
    if step < 0:
        return jnp.concatenate([zero, v[:-1]], axis=0)
    return jnp.concatenate([v[1:], zero], axis=0)


def store_cols(cols, f, h, v):
    for kz in range(3):
        moved = shift_z(v, kz - 1)
        for kw in range(3):
            lanes = slice((kw * 3 + kz) * C1, (kw * 3 + kz + 1) * C1)
            cols[f, (h + 1) * ROW : (h + 2) * ROW, lanes] = (
                shift_w(moved, kw - 1).reshape(ROW, C1).astype(jnp.bfloat16)
            )


def second_conv(n, far, meta, cols2, w2s, y2, outs):
    frames = cols2.shape[0]
    me = lax.axis_index("frame")
    half = CELLS // 2
    count = CELLS // n
    side = me // (n // 2)
    first = (1 - side if far else side) * half
    for f in range(frames):
        acc = jnp.zeros((half, C2), jnp.float32)
        for kh in range(3):
            start = pl.multiple_of(first + kh * ROW, ROW)
            acc = acc + jnp.dot(
                cols2[f, pl.ds(start, half), :], w2s[kh], preferred_element_type=jnp.float32
            )
        valid = jnp.where(me * frames + f < meta[0], 1.0, 0.0)
        y2[f * half : (f + 1) * half, :] = (silu(acc) * valid).astype(jnp.bfloat16)
    for f in range(frames):
        for k in range(n // 2):
            at = (me ^ (k + n // 2 if far else k)) % (n // 2)
            start = pl.multiple_of(f * half + at * count, count)
            block = y2[pl.ds(start, count), :]
            if far:
                outs[k][f] = block[: count // 2]
                outs[k + n // 2][f] = block[count // 2 :]
            else:
                outs[k][f] = block


def conv_kernel(n, meta, occ_hbm, w1_hbm, w2_hbm, *rest):
    outs = rest[:n]
    cols2, w2s = rest[n : n + 2]
    occ, w1, w2, t1, t2, w1s, cols1, y1, y2, sems = rest[n + 2 :]
    frames = occ.shape[0]
    bf16 = jnp.bfloat16

    copies = [pltpu.make_async_copy(w1_hbm, w1, sems.at[0])]
    for f in range(frames):
        copies.append(pltpu.make_async_copy(occ_hbm.at[0, f], occ.at[f], sems.at[1 + f]))
    for half in range(2):
        rows = slice(half * 128, half * 128 + 128)
        copies.append(
            pltpu.make_async_copy(w2_hbm.at[rows, :], w2.at[rows, :], sems.at[1 + frames + half])
        )
    for copy in copies:
        copy.start()
    cols1[:, 0:ROW, :] = jnp.zeros((frames, ROW, cols1.shape[2]), bf16)
    edge = jnp.zeros((frames, ROW, cols2.shape[2]), bf16)
    cols2[:, 0:ROW, :] = edge
    cols2[:, (ROWS + 1) * ROW :, :] = edge
    zero = jnp.zeros((CIN, C1), bf16)

    copies[0].wait()
    t1[...] = w1[...].astype(jnp.float32)
    for kz in range(3):

        def tap1(kh, kw):
            return t1[pl.ds(kh * 9 + kw * 3 + kz, CIN, stride=27), :].astype(bf16)

        for place, (kw, hp) in enumerate([(1, 0), (1, 1), (2, 0), (2, 1), (0, 0), (0, 1)]):
            rows = slice(kz * 384 + place * CIN, kz * 384 + place * CIN + CIN)
            w1s[rows, 0:C1] = tap1(hp + 1, kw)
            w1s[rows, C1 : 2 * C1] = tap1(0, kw) if hp == 1 else zero

    def columns(f):
        for h in range(ROWS):
            upper = occ[f, :, h * 256 : h * 256 + 128]
            lower = occ[f, :, h * 256 + 128 : h * 256 + 256]
            tile = jnp.concatenate([upper, lower], axis=0).astype(jnp.float32).T
            tile = tile.reshape(8, 2, ZD, 128)
            even, odd = tile[:, 0], tile[:, 1]
            for kz in range(3):
                e, o = shift_z(even, kz - 1), shift_z(odd, kz - 1)
                parts = (e, o, shift_w(o, -1))
                for i, part in enumerate(parts):
                    lanes = slice(kz * 384 + i * 128, kz * 384 + i * 128 + 128)
                    cols1[f, (h + 1) * ROW : (h + 2) * ROW, lanes] = part.reshape(ROW, 128).astype(bf16)

    def widen(f):
        for h in range(ROWS):
            v = (
                y1[f, (h + 1) * ROW : (h + 2) * ROW, 0:C1]
                + y1[f, h * ROW : (h + 1) * ROW, C1 : 2 * C1]
            )
            store_cols(cols2, f, h, silu(v).reshape(8, ZD, C1))

    pieces = w2.shape[1] // 128
    parts = max(frames - 1, 1)
    middle = (ROWS + 1) // 2 * ROW
    for copy in copies[1 : 1 + frames]:
        copy.wait()
    columns(0)
    for f in range(frames):
        part = f - (frames - parts)
        if part == 0:
            copies[1 + frames].wait()
            copies[2 + frames].wait()
        for rows in (slice(0, middle), slice(middle, (ROWS + 1) * ROW)):
            y1[f, rows, :] = jnp.dot(cols1[f, rows, :], w1s[...], preferred_element_type=jnp.float32)
        if f + 1 < frames:
            columns(f + 1)
        for j in range(max(part, 0) * pieces // parts, max(part + 1, 0) * pieces // parts):
            for half in range(2):
                t2[half, j * 128 : j * 128 + 128, :] = (
                    w2[half * 128 : half * 128 + 128, j * 128 : j * 128 + 128].astype(jnp.float32).T
                )
        widen(f)
    for kh in range(3):
        for kw in range(3):
            for kz in range(3):
                rows = slice((kw * 3 + kz) * C1, (kw * 3 + kz + 1) * C1)
                for half in range(2):
                    w2s[kh, rows, half * 128 : half * 128 + 128] = t2[
                        half, pl.ds(kh * 9 + kw * 3 + kz, C1, stride=27), :
                    ].astype(bf16)
    second_conv(n, True, meta, cols2, w2s, y2, outs)


def near_kernel(n, meta, cols2, w2s, *rest):
    second_conv(n, False, meta, cols2, w2s, rest[n // 2], rest[: n // 2])


def conv_far(n, meta, occ, w1, w2):
    frames = occ.shape[1]
    count = CELLS // n
    vmem = pl.BlockSpec(memory_space=pltpu.VMEM)
    hbm = pl.BlockSpec(memory_space=pltpu.HBM)
    f32, bf16 = jnp.float32, jnp.bfloat16
    res = pl.pallas_call(
        functools.partial(conv_kernel, n),
        out_shape=[jax.ShapeDtypeStruct((frames, count // 2, C2), bf16)] * n
        + [
            jax.ShapeDtypeStruct((frames, (ROWS + 2) * ROW, 9 * C1), bf16),
            jax.ShapeDtypeStruct((3, 9 * C1, C2), bf16),
        ],
        in_specs=[pl.BlockSpec(memory_space=pltpu.SMEM), hbm, hbm, hbm],
        out_specs=[vmem] * (n + 2),
        scratch_shapes=[
            pltpu.VMEM((frames, CIN, HI * HI * ZD), bf16),
            pltpu.VMEM((CIN * 27, C1), bf16),
            pltpu.VMEM((C2, C1 * 27), bf16),
            pltpu.VMEM((CIN * 27, C1), f32),
            pltpu.VMEM((2, C1 * 27, 128), f32),
            pltpu.VMEM((1152, 2 * C1), bf16),
            pltpu.VMEM((frames, (ROWS + 1) * ROW, 1152), bf16),
            pltpu.VMEM((frames, (ROWS + 1) * ROW, 2 * C1), f32),
            pltpu.VMEM((frames * CELLS // 2, C2), bf16),
            pltpu.SemaphoreType.DMA((3 + frames,)),
        ],
        compiler_params=pltpu.CompilerParams(vmem_limit_bytes=40 << 20),
        cost_estimate=pl.CostEstimate(
            flops=2 * frames * CELLS * (C1 * CIN * 27 + C2 * C1 * 27 // 2),
            bytes_accessed=4_000_000,
            transcendentals=frames * CELLS * (C1 + C2),
        ),
    )(meta, *[pltpu.with_memory_space_constraint(x, pltpu.HBM) for x in (occ, w1, w2)])
    return res[: n // 2], res[n // 2 : n], res[n], res[n + 1]


def conv_near(n, meta, cols2, w2s):
    frames = cols2.shape[0]
    count = CELLS // n
    vmem = pl.BlockSpec(memory_space=pltpu.VMEM)
    return pl.pallas_call(
        functools.partial(near_kernel, n),
        out_shape=[jax.ShapeDtypeStruct((frames, count, C2), jnp.bfloat16)] * (n // 2),
        in_specs=[pl.BlockSpec(memory_space=pltpu.SMEM), vmem, vmem],
        out_specs=[vmem] * (n // 2),
        scratch_shapes=[pltpu.VMEM((frames * CELLS // 2, C2), jnp.bfloat16)],
        compiler_params=pltpu.CompilerParams(vmem_limit_bytes=VMEM_LIMIT),
        cost_estimate=pl.CostEstimate(
            flops=2 * frames * CELLS * C2 * C1 * 27 // 2,
            bytes_accessed=4_000_000,
            transcendentals=frames * CELLS * C2 // 2,
        ),
    )(meta, cols2, w2s)


def nt_dot(a, b):
    return lax.dot_general(a, b, (((1,), (1,)), ((), ())), preferred_element_type=jnp.float32)


def swap_cells(even, odd):
    upper = lax.broadcasted_iota(jnp.int32, even.shape, even.ndim - 2) < 4
    low = jnp.where(upper, even, pltpu.roll(odd, 4, odd.ndim - 2))
    high = jnp.where(upper, pltpu.roll(even, 4, even.ndim - 2), odd)
    return low, high


def attend_kernel(n, half, meta, *rest):
    blocks = rest[:n]
    tw, wq, wk, wv, wo, before = rest[n : n + 6]
    rest = rest[n + 6 :]
    kept, rest = rest[: n // 2 * half], rest[n // 2 * half :]
    outs, squares = rest[:n], rest[n]
    seen, resid, q_s, k_s, v_s, a_s, kb, vb, p_s, bias, s_s, ones = rest[n + 1 :]
    me, length = lax.axis_index("frame"), meta[0]
    frames, count = blocks[0].shape[0], blocks[0].shape[1] // HALVES
    first_cell = [half * count if k < n // 2 else 0 for k in range(n)]
    groups = count // 8
    total = n * frames
    rows = total * 4
    f32, bf16 = jnp.float32, jnp.bfloat16
    head_of = lax.broadcasted_iota(jnp.int32, (rows, C2), 1) // HD

    edge = jnp.zeros((groups, 1, 8, C2), f32)
    seen[:, 0:1] = edge
    seen[:, total + 1 : total + 2] = edge
    for k in range(n):
        first = (me ^ k) * frames + 1
        for f in range(frames):
            tile = blocks[k][f, first_cell[k] : first_cell[k] + count, :]
            tile = tile.astype(f32).reshape(groups, 8, C2)
            for g in range(groups):
                seen[g, first + f] = tile[g]

    at = lax.broadcasted_iota(jnp.int32, (rows, rows), 0)
    to = lax.broadcasted_iota(jnp.int32, (rows, rows), 1)
    bias[...] = jnp.where((at & 3 == to & 3) & (to >> 2 < length), 0.0, NEG)
    for h in range(HEADS):
        ones[h * rows : (h + 1) * rows, :] = jnp.where(head_of == h, 1.0, 0.0).astype(bf16)
    valid = lax.broadcasted_iota(jnp.int32, (rows, C2), 0) >> 2 < length
    none = jnp.zeros((rows, C2), bf16)

    def project(g):
        summed = jnp.zeros((total * 8, C2), f32)
        for j in range(3):
            mix = seen[g, j : j + total].reshape(total * 8, C2).astype(bf16)
            summed = summed + nt_dot(mix, tw[j])
        res = (seen[g, 1 : total + 1].reshape(total * 8, C2) + silu(summed)).astype(bf16)
        res = res.astype(f32).reshape(total // 2, 2, 8, C2)
        for part, value in enumerate(swap_cells(res[:, 0], res[:, 1])):
            value = value.reshape(rows, C2)
            start = (2 * g + part) * rows
            resid[start : start + rows, :] = value
            mean = jnp.sum(value * value, axis=1, keepdims=True) * (1.0 / C2)
            a_s[start : start + rows, :] = (value * lax.rsqrt(mean + NORM_EPS)).astype(bf16)

    def qkv(start, size):
        some = slice(start, start + size)
        q_s[some, :] = (nt_dot(a_s[some, :], wq[...]).astype(bf16) * HD ** (-0.5)).astype(bf16)
        k_s[some, :] = nt_dot(a_s[some, :], wk[...]).astype(bf16)
        v_s[some, :] = nt_dot(a_s[some, :], wv[...]).astype(bf16)

    def score(b):
        here = slice(b * rows, (b + 1) * rows)
        keys, values = k_s[here, :], v_s[here, :]
        for h in range(HEADS):
            kb[b % 3, h * rows : (h + 1) * rows, :] = jnp.where(head_of == h, keys, none)
            vb[b % 3, h * rows : (h + 1) * rows, :] = jnp.where(head_of == h, values, none)
        s_s[b % 3] = nt_dot(q_s[here, :], kb[b % 3])

    def soften(b):
        for h in range(HEADS):
            mine = s_s[b % 3, :, h * rows : (h + 1) * rows] + bias[...]
            top = jnp.max(mine, axis=1, keepdims=True)
            p_s[b % 3, :, h * rows : (h + 1) * rows] = jnp.exp(mine - top).astype(bf16)

    def weigh(b):
        here = slice(b * rows, (b + 1) * rows)
        weighted = jnp.dot(p_s[b % 3], vb[b % 3], preferred_element_type=f32)
        sums = jnp.dot(p_s[b % 3], ones[...], preferred_element_type=f32)
        a_s[here, :] = (weighted / sums).astype(bf16)

    def emit(g):
        parts = []
        add = jnp.zeros((8, C2), f32)
        for part in range(2):
            here = slice((2 * g + part) * rows, (2 * g + part + 1) * rows)
            full = resid[here, :] + nt_dot(a_s[here, :], wo[...])
            full = jnp.where(valid, full, 0.0).astype(bf16).astype(f32)
            add = add + jnp.sum((full * full).reshape(rows // 8, 8, C2), axis=0)
            parts.append(full.reshape(total // 2, 8, C2))
        squares[...] = squares[...] + add
        even, odd = swap_cells(*parts)
        seen[g, 0:total] = jnp.stack([even, odd], axis=1).reshape(total, 8, C2)

    squares[...] = before[...]
    last = 2 * groups - 1
    for g in range(groups):
        project(g)
    for b in range(0, 2 * groups, 4):
        qkv(b * rows, min(4, 2 * groups - b) * rows)
    score(0)
    for b in range(2 * groups):
        if b < last:
            score(b + 1)
        soften(b)
        if b > 0:
            weigh(b - 1)
        if b > 1 and b % 2 == 0:
            emit(b // 2 - 1)
    weigh(last)
    emit(groups - 1)

    for k in range(n):
        first = (me ^ k) * frames
        at = 0
        if half == 1 and k < n // 2:
            outs[k][0 : frames * count, :] = kept[k][...]
            at = frames * count
        for f in range(frames):
            tile = jnp.concatenate([seen[g, first + f] for g in range(groups)], axis=0)
            outs[k][at + f * count : at + (f + 1) * count, :] = tile.astype(bf16)
    if half == 1:
        sum_of = jnp.broadcast_to(jnp.sum(squares[...], keepdims=True), (TAIL, C2))
        row = lax.broadcasted_iota(jnp.int32, (TAIL, C2), 0)
        high = sum_of.astype(bf16).astype(f32)
        middle = (sum_of - high).astype(bf16).astype(f32)
        low = sum_of - high - middle
        tail = jnp.where(row == 0, high, jnp.where(row == 1, middle, jnp.where(row == 2, low, 0.0)))
        for k in range(n):
            outs[k][outs[k].shape[0] - TAIL :, :] = tail.astype(bf16)


def attend(n, half, meta, blocks, weights, before, kept):
    frames, both, _ = blocks[0].shape
    count = both // HALVES
    total = n * frames
    rows = total * 4
    groups = count // 8
    everything = 2 * groups * rows
    vmem = pl.BlockSpec(memory_space=pltpu.VMEM)
    f32, bf16 = jnp.float32, jnp.bfloat16
    sizes = [frames * count] * n
    if half == 1:
        sizes = [frames * (both if k < n // 2 else count) + TAIL for k in range(n)]
    res = pl.pallas_call(
        functools.partial(attend_kernel, n, half),
        out_shape=[jax.ShapeDtypeStruct((size, C2), bf16) for size in sizes]
        + [jax.ShapeDtypeStruct((8, C2), f32)],
        in_specs=[pl.BlockSpec(memory_space=pltpu.SMEM)] + [vmem] * (n + 6 + len(kept)),
        out_specs=[vmem] * (n + 1),
        scratch_shapes=[
            pltpu.VMEM((groups, total + 2, 8, C2), f32),
            pltpu.VMEM((everything, C2), f32),
            pltpu.VMEM((everything, C2), bf16),
            pltpu.VMEM((everything, C2), bf16),
            pltpu.VMEM((everything, C2), bf16),
            pltpu.VMEM((everything, C2), bf16),
            pltpu.VMEM((3, HEADS * rows, C2), bf16),
            pltpu.VMEM((3, HEADS * rows, C2), bf16),
            pltpu.VMEM((3, rows, HEADS * rows), bf16),
            pltpu.VMEM((rows, rows), f32),
            pltpu.VMEM((3, rows, HEADS * rows), f32),
            pltpu.VMEM((HEADS * rows, C2), bf16),
        ],
        compiler_params=pltpu.CompilerParams(vmem_limit_bytes=VMEM_LIMIT),
        cost_estimate=pl.CostEstimate(
            flops=2 * everything * C2 * (7 * C2 + 12 * rows),
            bytes_accessed=4_000_000,
            transcendentals=everything * HEADS * rows,
        ),
    )(meta, *blocks, *weights, before, *kept)
    return res[:n], res[n]


def gather_kernel(n, *rest):
    early, late, out, whole = rest[: n // 2], rest[n // 2 : n // 2 + n], rest[-2], rest[-1]
    me = lax.axis_index("frame")
    frames = out.shape[0]
    count = CELLS // n
    part = count // HALVES
    for k in range(n):
        start = pl.multiple_of((me ^ k) * count, count)
        for half in range(HALVES):
            block, first = late[k], 0
            if k >= n // 2 and half == 0:
                block = early[k - n // 2]
            elif k < n // 2:
                first = half * frames * part
            for f in range(frames):
                rows = slice(first + f * part, first + (f + 1) * part)
                whole[f, pl.ds(start + half * part, part), :] = block[rows, :]
    for f in range(frames):
        out[f] = whole[f].astype(jnp.float32).T.astype(jnp.bfloat16)


def gather(n, frames, early, late):
    vmem = pl.BlockSpec(memory_space=pltpu.VMEM)
    return pl.pallas_call(
        functools.partial(gather_kernel, n),
        out_shape=jax.ShapeDtypeStruct((frames, C2, CELLS), jnp.bfloat16),
        in_specs=[vmem] * (len(early) + len(late)),
        out_specs=vmem,
        scratch_shapes=[pltpu.VMEM((frames, CELLS, C2), jnp.bfloat16)],
        compiler_params=pltpu.CompilerParams(vmem_limit_bytes=VMEM_LIMIT),
        cost_estimate=pl.CostEstimate(flops=0, bytes_accessed=4_000_000, transcendentals=0),
    )(*early, *late)


def tally_kernel(n, *rest):
    total = jnp.zeros((TAIL, C2), jnp.float32)
    for k in range(n):
        total = total + rest[k][...].astype(jnp.float32)
    rest[n][...] = jnp.broadcast_to(jnp.sum(total, axis=0, keepdims=True)[:, :128], (8, 128))


def last_tile(rows):
    return pl.BlockSpec((TAIL, C2), lambda i: (rows // TAIL - 1, 0))


def tally(n, blocks):
    return pl.pallas_call(
        functools.partial(tally_kernel, n),
        grid=(1,),
        out_shape=jax.ShapeDtypeStruct((8, 128), jnp.float32),
        in_specs=[last_tile(block.shape[0]) for block in blocks],
        out_specs=pl.BlockSpec((8, 128), lambda i: (0, 0)),
        compiler_params=pltpu.CompilerParams(vmem_limit_bytes=VMEM_LIMIT // 16),
        cost_estimate=pl.CostEstimate(flops=0, bytes_accessed=100_000, transcendentals=0),
    )(*blocks)


def finish_kernel(scale, mine, *rest):
    total = mine[...]
    for other in rest[:-1]:
        total = total + other[...]
    rest[-1][0, 0] = jnp.max(total) * scale


def finish(scale, mine, others):
    vmem = pl.BlockSpec(memory_space=pltpu.VMEM)
    return pl.pallas_call(
        functools.partial(finish_kernel, scale),
        out_shape=jax.ShapeDtypeStruct((1, 1), jnp.float32),
        in_specs=[vmem] * (1 + len(others)),
        out_specs=pl.BlockSpec(memory_space=pltpu.SMEM),
        compiler_params=pltpu.CompilerParams(vmem_limit_bytes=VMEM_LIMIT // 16),
        cost_estimate=pl.CostEstimate(flops=0, bytes_accessed=100_000, transcendentals=0),
    )(mine, *others)


def far_of(n):
    return list(range(n // 2, n))


def near_of(n):
    return list(range(1, n // 2))


def send(n, k, block):
    return lax.ppermute(block, "frame", [(i, i ^ k) for i in range(n)])


def shards(occ, lengths, w1, w2, tw, wq, wk, wv, wo):
    n = lax.axis_size("frame")
    scenes = lax.axis_size("scene")
    frames = occ.shape[1]
    weights = (tw, wq, wk, wv, wo)
    far0, far1, cols2, w2s = conv_far(n, lengths, occ, w1.T, w2)
    moved0, moved1 = [None] * n, [None] * n
    for k in far_of(n):
        moved0[k] = send(n, k, far0[k - n // 2])
    near = conv_near(n, lengths, cols2, w2s)
    moved0[0] = moved1[0] = near[0]
    for k in near_of(n):
        moved0[k] = moved1[k] = send(n, k, near[k])
    for k in far_of(n):
        moved1[k] = send(n, k, far1[k - n // 2])
    squares = jnp.zeros((8, C2), jnp.float32)
    first, squares = attend(n, 0, lengths, moved0, weights, squares, [])
    early = {k: send(n, k, first[k]) for k in far_of(n)}
    second, _ = attend(n, 1, lengths, moved1, weights, squares, list(first[: n // 2]))
    late = [second[0]] + [None] * (n - 1)
    for k in far_of(n) + near_of(n):
        late[k] = send(n, k, second[k])
    mine = tally(n, late)
    others = []
    for step in range(1, scenes):
        others.append(lax.ppermute(mine, "scene", [(i, i ^ step) for i in range(scenes)]))
    encoded = gather(n, frames, [early[k] for k in range(n // 2, n)], late)
    scale = 0.5 / float(scenes * n * frames * CELLS * C2)
    loss = finish(scale, mine, others)
    return (encoded[None], loss.reshape(()))


def solution(mesh):
    placed = (P("scene", "frame", None, None), P("scene"), P(), P(), P(), P(), P(), P(), P())
    return jax.shard_map(
        shards,
        mesh=mesh,
        in_specs=placed,
        out_specs=(P("scene", "frame", None, None), P()),
        check_vma=False,
    )
```

```python
import functools

import jax
import jax.numpy as jnp
from jax import lax
from jax.experimental import pallas as pl
from jax.experimental.pallas import tpu as pltpu
from jax.sharding import PartitionSpec as P


CIN = 64
C1 = 128
C2 = 256
HEADS = 4
HD = 64
HI = 16
ZD = 8
CELLS = 512
ROWS = 8
ROW = 64
HALVES = 2
NORM_EPS = 1e-06
NEG = -1e30
TAIL = 8
VMEM_LIMIT = 24 << 20


def silu(v):
    half = 0.5 * v
    return half + half * jnp.tanh(half)


def shift_z(v, step):
    if step == 0:
        return v
    z = lax.broadcasted_iota(jnp.int32, v.shape, v.ndim - 2)
    moved = pltpu.roll(v, (-step) % ZD, v.ndim - 2)
    keep = (z + step >= 0) & (z + step < ZD)
    return jnp.where(keep, moved, 0.0)


def shift_w(v, step):
    if step == 0:
        return v
    zero = jnp.zeros_like(v[:1])
    if step < 0:
        return jnp.concatenate([zero, v[:-1]], axis=0)
    return jnp.concatenate([v[1:], zero], axis=0)


def store_cols(cols, f, h, v):
    for kz in range(3):
        moved = shift_z(v, kz - 1)
        for kw in range(3):
            lanes = slice((kw * 3 + kz) * C1, (kw * 3 + kz + 1) * C1)
            cols[f, (h + 1) * ROW : (h + 2) * ROW, lanes] = (
                shift_w(moved, kw - 1).reshape(ROW, C1).astype(jnp.bfloat16)
            )


def second_conv(n, far, meta, cols2, w2s, y2, outs):
    frames = cols2.shape[0]
    me = lax.axis_index("frame")
    half = CELLS // 2
    count = CELLS // n
    side = me // (n // 2)
    first = (1 - side if far else side) * half
    for f in range(frames):
        acc = jnp.zeros((half, C2), jnp.float32)
        for kh in range(3):
            start = pl.multiple_of(first + kh * ROW, ROW)
            acc = acc + jnp.dot(
                cols2[f, pl.ds(start, half), :], w2s[kh], preferred_element_type=jnp.float32
            )
        valid = jnp.where(me * frames + f < meta[0], 1.0, 0.0)
        y2[f * half : (f + 1) * half, :] = (silu(acc) * valid).astype(jnp.bfloat16)
    for f in range(frames):
        for k in range(n // 2):
            at = (me ^ (k + n // 2 if far else k)) % (n // 2)
            start = pl.multiple_of(f * half + at * count, count)
            block = y2[pl.ds(start, count), :]
            if far:
                outs[k][f] = block[: count // 2]
                outs[k + n // 2][f] = block[count // 2 :]
            else:
                outs[k][f] = block


def conv_kernel(n, meta, occ_hbm, w1_hbm, w2_hbm, *rest):
    outs = rest[:n]
    cols2, w2s = rest[n : n + 2]
    occ, w1, w2, t1, t2, w1s, cols1, y1, y2, sems = rest[n + 2 :]
    frames = occ.shape[0]
    bf16 = jnp.bfloat16

    copies = [pltpu.make_async_copy(w1_hbm, w1, sems.at[0])]
    for f in range(frames):
        copies.append(pltpu.make_async_copy(occ_hbm.at[0, f], occ.at[f], sems.at[1 + f]))
    for half in range(2):
        rows = slice(half * 128, half * 128 + 128)
        copies.append(
            pltpu.make_async_copy(w2_hbm.at[rows, :], w2.at[rows, :], sems.at[1 + frames + half])
        )
    for copy in copies:
        copy.start()
    cols1[:, 0:ROW, :] = jnp.zeros((frames, ROW, cols1.shape[2]), bf16)
    edge = jnp.zeros((frames, ROW, cols2.shape[2]), bf16)
    cols2[:, 0:ROW, :] = edge
    cols2[:, (ROWS + 1) * ROW :, :] = edge
    zero = jnp.zeros((CIN, C1), bf16)

    copies[0].wait()
    t1[...] = w1[...].astype(jnp.float32)
    for kz in range(3):

        def tap1(kh, kw):
            return t1[pl.ds(kh * 9 + kw * 3 + kz, CIN, stride=27), :].astype(bf16)

        for place, (kw, hp) in enumerate([(1, 0), (1, 1), (2, 0), (2, 1), (0, 0), (0, 1)]):
            rows = slice(kz * 384 + place * CIN, kz * 384 + place * CIN + CIN)
            w1s[rows, 0:C1] = tap1(hp + 1, kw)
            w1s[rows, C1 : 2 * C1] = tap1(0, kw) if hp == 1 else zero

    def columns(f):
        for h in range(ROWS):
            upper = occ[f, :, h * 256 : h * 256 + 128]
            lower = occ[f, :, h * 256 + 128 : h * 256 + 256]
            tile = jnp.concatenate([upper, lower], axis=0).astype(jnp.float32).T
            tile = tile.reshape(8, 2, ZD, 128)
            even, odd = tile[:, 0], tile[:, 1]
            for kz in range(3):
                e, o = shift_z(even, kz - 1), shift_z(odd, kz - 1)
                parts = (e, o, shift_w(o, -1))
                for i, part in enumerate(parts):
                    lanes = slice(kz * 384 + i * 128, kz * 384 + i * 128 + 128)
                    cols1[f, (h + 1) * ROW : (h + 2) * ROW, lanes] = part.reshape(ROW, 128).astype(bf16)

    def widen(f):
        for h in range(ROWS):
            v = (
                y1[f, (h + 1) * ROW : (h + 2) * ROW, 0:C1]
                + y1[f, h * ROW : (h + 1) * ROW, C1 : 2 * C1]
            )
            store_cols(cols2, f, h, silu(v).reshape(8, ZD, C1))

    pieces = w2.shape[1] // 128
    parts = max(frames - 1, 1)
    middle = (ROWS + 1) // 2 * ROW
    for copy in copies[1 : 1 + frames]:
        copy.wait()
    columns(0)
    for f in range(frames):
        part = f - (frames - parts)
        if part == 0:
            copies[1 + frames].wait()
            copies[2 + frames].wait()
        for rows in (slice(0, middle), slice(middle, (ROWS + 1) * ROW)):
            y1[f, rows, :] = jnp.dot(cols1[f, rows, :], w1s[...], preferred_element_type=jnp.float32)
        if f + 1 < frames:
            columns(f + 1)
        for j in range(max(part, 0) * pieces // parts, max(part + 1, 0) * pieces // parts):
            for half in range(2):
                t2[half, j * 128 : j * 128 + 128, :] = (
                    w2[half * 128 : half * 128 + 128, j * 128 : j * 128 + 128].astype(jnp.float32).T
                )
        widen(f)
    for kh in range(3):
        for kw in range(3):
            for kz in range(3):
                rows = slice((kw * 3 + kz) * C1, (kw * 3 + kz + 1) * C1)
                for half in range(2):
                    w2s[kh, rows, half * 128 : half * 128 + 128] = t2[
                        half, pl.ds(kh * 9 + kw * 3 + kz, C1, stride=27), :
                    ].astype(bf16)
    second_conv(n, True, meta, cols2, w2s, y2, outs)


def near_kernel(n, meta, cols2, w2s, *rest):
    second_conv(n, False, meta, cols2, w2s, rest[n // 2], rest[: n // 2])


def conv_far(n, meta, occ, w1, w2):
    frames = occ.shape[1]
    count = CELLS // n
    vmem = pl.BlockSpec(memory_space=pltpu.VMEM)
    hbm = pl.BlockSpec(memory_space=pltpu.HBM)
    f32, bf16 = jnp.float32, jnp.bfloat16
    res = pl.pallas_call(
        functools.partial(conv_kernel, n),
        out_shape=[jax.ShapeDtypeStruct((frames, count // 2, C2), bf16)] * n
        + [
            jax.ShapeDtypeStruct((frames, (ROWS + 2) * ROW, 9 * C1), bf16),
            jax.ShapeDtypeStruct((3, 9 * C1, C2), bf16),
        ],
        in_specs=[pl.BlockSpec(memory_space=pltpu.SMEM), hbm, hbm, hbm],
        out_specs=[vmem] * (n + 2),
        scratch_shapes=[
            pltpu.VMEM((frames, CIN, HI * HI * ZD), bf16),
            pltpu.VMEM((CIN * 27, C1), bf16),
            pltpu.VMEM((C2, C1 * 27), bf16),
            pltpu.VMEM((CIN * 27, C1), f32),
            pltpu.VMEM((2, C1 * 27, 128), f32),
            pltpu.VMEM((1152, 2 * C1), bf16),
            pltpu.VMEM((frames, (ROWS + 1) * ROW, 1152), bf16),
            pltpu.VMEM((frames, (ROWS + 1) * ROW, 2 * C1), f32),
            pltpu.VMEM((frames * CELLS // 2, C2), bf16),
            pltpu.SemaphoreType.DMA((3 + frames,)),
        ],
        compiler_params=pltpu.CompilerParams(vmem_limit_bytes=40 << 20),
        cost_estimate=pl.CostEstimate(
            flops=2 * frames * CELLS * (C1 * CIN * 27 + C2 * C1 * 27 // 2),
            bytes_accessed=4_000_000,
            transcendentals=frames * CELLS * (C1 + C2),
        ),
    )(meta, *[pltpu.with_memory_space_constraint(x, pltpu.HBM) for x in (occ, w1, w2)])
    return res[: n // 2], res[n // 2 : n], res[n], res[n + 1]


def conv_near(n, meta, cols2, w2s):
    frames = cols2.shape[0]
    count = CELLS // n
    vmem = pl.BlockSpec(memory_space=pltpu.VMEM)
    return pl.pallas_call(
        functools.partial(near_kernel, n),
        out_shape=[jax.ShapeDtypeStruct((frames, count, C2), jnp.bfloat16)] * (n // 2),
        in_specs=[pl.BlockSpec(memory_space=pltpu.SMEM), vmem, vmem],
        out_specs=[vmem] * (n // 2),
        scratch_shapes=[pltpu.VMEM((frames * CELLS // 2, C2), jnp.bfloat16)],
        compiler_params=pltpu.CompilerParams(vmem_limit_bytes=VMEM_LIMIT),
        cost_estimate=pl.CostEstimate(
            flops=2 * frames * CELLS * C2 * C1 * 27 // 2,
            bytes_accessed=4_000_000,
            transcendentals=frames * CELLS * C2 // 2,
        ),
    )(meta, cols2, w2s)


def nt_dot(a, b):
    return lax.dot_general(a, b, (((1,), (1,)), ((), ())), preferred_element_type=jnp.float32)


def swap_cells(even, odd):
    upper = lax.broadcasted_iota(jnp.int32, even.shape, even.ndim - 2) < 4
    low = jnp.where(upper, even, pltpu.roll(odd, 4, odd.ndim - 2))
    high = jnp.where(upper, pltpu.roll(even, 4, even.ndim - 2), odd)
    return low, high


def attend_kernel(n, half, meta, *rest):
    blocks = rest[:n]
    tw, wq, wk, wv, wo, before = rest[n : n + 6]
    rest = rest[n + 6 :]
    kept, rest = rest[: n // 2 * half], rest[n // 2 * half :]
    outs, squares = rest[:n], rest[n]
    seen, resid, q_s, k_s, v_s, a_s, kb, vb, p_s, bias, s_s, ones = rest[n + 1 :]
    me, length = lax.axis_index("frame"), meta[0]
    frames, count = blocks[0].shape[0], blocks[0].shape[1] // HALVES
    first_cell = [half * count if k < n // 2 else 0 for k in range(n)]
    groups = count // 8
    total = n * frames
    rows = total * 4
    f32, bf16 = jnp.float32, jnp.bfloat16
    head_of = lax.broadcasted_iota(jnp.int32, (rows, C2), 1) // HD

    edge = jnp.zeros((groups, 1, 8, C2), f32)
    seen[:, 0:1] = edge
    seen[:, total + 1 : total + 2] = edge
    for k in range(n):
        first = (me ^ k) * frames + 1
        for f in range(frames):
            tile = blocks[k][f, first_cell[k] : first_cell[k] + count, :]
            tile = tile.astype(f32).reshape(groups, 8, C2)
            for g in range(groups):
                seen[g, first + f] = tile[g]

    at = lax.broadcasted_iota(jnp.int32, (rows, rows), 0)
    to = lax.broadcasted_iota(jnp.int32, (rows, rows), 1)
    bias[...] = jnp.where((at & 3 == to & 3) & (to >> 2 < length), 0.0, NEG)
    for h in range(HEADS):
        ones[h * rows : (h + 1) * rows, :] = jnp.where(head_of == h, 1.0, 0.0).astype(bf16)
    valid = lax.broadcasted_iota(jnp.int32, (rows, C2), 0) >> 2 < length
    none = jnp.zeros((rows, C2), bf16)

    def project(g):
        summed = jnp.zeros((total * 8, C2), f32)
        for j in range(3):
            mix = seen[g, j : j + total].reshape(total * 8, C2).astype(bf16)
            summed = summed + nt_dot(mix, tw[j])
        res = (seen[g, 1 : total + 1].reshape(total * 8, C2) + silu(summed)).astype(bf16)
        res = res.astype(f32).reshape(total // 2, 2, 8, C2)
        for part, value in enumerate(swap_cells(res[:, 0], res[:, 1])):
            value = value.reshape(rows, C2)
            start = (2 * g + part) * rows
            resid[start : start + rows, :] = value
            mean = jnp.sum(value * value, axis=1, keepdims=True) * (1.0 / C2)
            a_s[start : start + rows, :] = (value * lax.rsqrt(mean + NORM_EPS)).astype(bf16)

    def qkv(start, size):
        some = slice(start, start + size)
        q_s[some, :] = (nt_dot(a_s[some, :], wq[...]).astype(bf16) * HD ** (-0.5)).astype(bf16)
        k_s[some, :] = nt_dot(a_s[some, :], wk[...]).astype(bf16)
        v_s[some, :] = nt_dot(a_s[some, :], wv[...]).astype(bf16)

    def score(b):
        here = slice(b * rows, (b + 1) * rows)
        keys, values = k_s[here, :], v_s[here, :]
        for h in range(HEADS):
            kb[b % 3, h * rows : (h + 1) * rows, :] = jnp.where(head_of == h, keys, none)
            vb[b % 3, h * rows : (h + 1) * rows, :] = jnp.where(head_of == h, values, none)
        s_s[b % 3] = nt_dot(q_s[here, :], kb[b % 3])

    def soften(b):
        for h in range(HEADS):
            mine = s_s[b % 3, :, h * rows : (h + 1) * rows] + bias[...]
            top = jnp.max(mine, axis=1, keepdims=True)
            p_s[b % 3, :, h * rows : (h + 1) * rows] = jnp.exp(mine - top).astype(bf16)

    def weigh(b):
        here = slice(b * rows, (b + 1) * rows)
        weighted = jnp.dot(p_s[b % 3], vb[b % 3], preferred_element_type=f32)
        sums = jnp.dot(p_s[b % 3], ones[...], preferred_element_type=f32)
        a_s[here, :] = (weighted / sums).astype(bf16)

    def emit(g):
        parts = []
        add = jnp.zeros((8, C2), f32)
        for part in range(2):
            here = slice((2 * g + part) * rows, (2 * g + part + 1) * rows)
            full = resid[here, :] + nt_dot(a_s[here, :], wo[...])
            full = jnp.where(valid, full, 0.0).astype(bf16).astype(f32)
            add = add + jnp.sum((full * full).reshape(rows // 8, 8, C2), axis=0)
            parts.append(full.reshape(total // 2, 8, C2))
        squares[...] = squares[...] + add
        even, odd = swap_cells(*parts)
        seen[g, 0:total] = jnp.stack([even, odd], axis=1).reshape(total, 8, C2)

    squares[...] = before[...]
    last = 2 * groups - 1
    for g in range(groups):
        project(g)
    for b in range(0, 2 * groups, 4):
        qkv(b * rows, min(4, 2 * groups - b) * rows)
    score(0)
    for b in range(2 * groups):
        if b < last:
            score(b + 1)
        soften(b)
        if b > 0:
            weigh(b - 1)
        if b > 1 and b % 2 == 0:
            emit(b // 2 - 1)
    weigh(last)
    emit(groups - 1)

    for k in range(n):
        first = (me ^ k) * frames
        at = 0
        if half == 1 and k < n // 2:
            outs[k][0 : frames * count, :] = kept[k][...]
            at = frames * count
        for f in range(frames):
            tile = jnp.concatenate([seen[g, first + f] for g in range(groups)], axis=0)
            outs[k][at + f * count : at + (f + 1) * count, :] = tile.astype(bf16)
    if half == 1:
        sum_of = jnp.broadcast_to(jnp.sum(squares[...], keepdims=True), (TAIL, C2))
        row = lax.broadcasted_iota(jnp.int32, (TAIL, C2), 0)
        high = sum_of.astype(bf16).astype(f32)
        middle = (sum_of - high).astype(bf16).astype(f32)
        low = sum_of - high - middle
        tail = jnp.where(row == 0, high, jnp.where(row == 1, middle, jnp.where(row == 2, low, 0.0)))
        for k in range(n):
            outs[k][outs[k].shape[0] - TAIL :, :] = tail.astype(bf16)


def attend(n, half, meta, blocks, weights, before, kept):
    frames, both, _ = blocks[0].shape
    count = both // HALVES
    total = n * frames
    rows = total * 4
    groups = count // 8
    everything = 2 * groups * rows
    vmem = pl.BlockSpec(memory_space=pltpu.VMEM)
    f32, bf16 = jnp.float32, jnp.bfloat16
    sizes = [frames * count] * n
    if half == 1:
        sizes = [frames * (both if k < n // 2 else count) + TAIL for k in range(n)]
    res = pl.pallas_call(
        functools.partial(attend_kernel, n, half),
        out_shape=[jax.ShapeDtypeStruct((size, C2), bf16) for size in sizes]
        + [jax.ShapeDtypeStruct((8, C2), f32)] * (1 - half),
        in_specs=[pl.BlockSpec(memory_space=pltpu.SMEM)] + [vmem] * (n + 6 + len(kept)),
        out_specs=[vmem] * (n + 1 - half),
        scratch_shapes=[pltpu.VMEM((8, C2), f32)] * half
        + [
            pltpu.VMEM((groups, total + 2, 8, C2), f32),
            pltpu.VMEM((everything, C2), f32),
            pltpu.VMEM((everything, C2), bf16),
            pltpu.VMEM((everything, C2), bf16),
            pltpu.VMEM((everything, C2), bf16),
            pltpu.VMEM((everything, C2), bf16),
            pltpu.VMEM((3, HEADS * rows, C2), bf16),
            pltpu.VMEM((3, HEADS * rows, C2), bf16),
            pltpu.VMEM((3, rows, HEADS * rows), bf16),
            pltpu.VMEM((rows, rows), f32),
            pltpu.VMEM((3, rows, HEADS * rows), f32),
            pltpu.VMEM((HEADS * rows, C2), bf16),
        ],
        compiler_params=pltpu.CompilerParams(vmem_limit_bytes=VMEM_LIMIT),
        cost_estimate=pl.CostEstimate(
            flops=2 * everything * C2 * (7 * C2 + 12 * rows),
            bytes_accessed=4_000_000,
            transcendentals=everything * HEADS * rows,
        ),
    )(meta, *blocks, *weights, before, *kept)
    return res[:n], res[-1]


def gather_kernel(n, *rest):
    early, late, out, whole = rest[: n // 2], rest[n // 2 : n // 2 + n], rest[-2], rest[-1]
    me = lax.axis_index("frame")
    frames = out.shape[0]
    count = CELLS // n
    part = count // HALVES
    for k in range(n):
        start = pl.multiple_of((me ^ k) * count, count)
        for half in range(HALVES):
            block, first = late[k], 0
            if k >= n // 2 and half == 0:
                block = early[k - n // 2]
            elif k < n // 2:
                first = half * frames * part
            for f in range(frames):
                rows = slice(first + f * part, first + (f + 1) * part)
                whole[f, pl.ds(start + half * part, part), :] = block[rows, :]
    for f in range(frames):
        out[f] = whole[f].astype(jnp.float32).T.astype(jnp.bfloat16)


def gather(n, frames, early, late):
    vmem = pl.BlockSpec(memory_space=pltpu.VMEM)
    return pl.pallas_call(
        functools.partial(gather_kernel, n),
        out_shape=jax.ShapeDtypeStruct((frames, C2, CELLS), jnp.bfloat16),
        in_specs=[vmem] * (len(early) + len(late)),
        out_specs=vmem,
        scratch_shapes=[pltpu.VMEM((frames, CELLS, C2), jnp.bfloat16)],
        compiler_params=pltpu.CompilerParams(vmem_limit_bytes=VMEM_LIMIT),
        cost_estimate=pl.CostEstimate(flops=0, bytes_accessed=4_000_000, transcendentals=0),
    )(*early, *late)


def tally_kernel(n, *rest):
    total = jnp.zeros((TAIL, C2), jnp.float32)
    for k in range(n):
        total = total + rest[k][...].astype(jnp.float32)
    rest[n][...] = jnp.broadcast_to(jnp.sum(total, axis=0, keepdims=True)[:, :128], (8, 128))


def last_tile(rows):
    return pl.BlockSpec((TAIL, C2), lambda i: (rows // TAIL - 1, 0))


def tally(n, blocks):
    return pl.pallas_call(
        functools.partial(tally_kernel, n),
        grid=(1,),
        out_shape=jax.ShapeDtypeStruct((8, 128), jnp.float32),
        in_specs=[last_tile(block.shape[0]) for block in blocks],
        out_specs=pl.BlockSpec((8, 128), lambda i: (0, 0)),
        compiler_params=pltpu.CompilerParams(vmem_limit_bytes=VMEM_LIMIT // 16),
        cost_estimate=pl.CostEstimate(flops=0, bytes_accessed=100_000, transcendentals=0),
    )(*blocks)


def finish_kernel(scale, mine, *rest):
    total = mine[...]
    for other in rest[:-1]:
        total = total + other[...]
    rest[-1][0, 0] = jnp.max(total) * scale


def finish(scale, mine, others):
    vmem = pl.BlockSpec(memory_space=pltpu.VMEM)
    return pl.pallas_call(
        functools.partial(finish_kernel, scale),
        out_shape=jax.ShapeDtypeStruct((1, 1), jnp.float32),
        in_specs=[vmem] * (1 + len(others)),
        out_specs=pl.BlockSpec(memory_space=pltpu.SMEM),
        compiler_params=pltpu.CompilerParams(vmem_limit_bytes=VMEM_LIMIT // 16),
        cost_estimate=pl.CostEstimate(flops=0, bytes_accessed=100_000, transcendentals=0),
    )(mine, *others)


def far_of(n):
    return list(range(n // 2, n))


def near_of(n):
    return list(range(1, n // 2))


def send(n, k, block):
    return lax.ppermute(block, "frame", [(i, i ^ k) for i in range(n)])


def shards(occ, lengths, w1, w2, tw, wq, wk, wv, wo):
    n = lax.axis_size("frame")
    scenes = lax.axis_size("scene")
    frames = occ.shape[1]
    weights = (tw, wq, wk, wv, wo)
    far0, far1, cols2, w2s = conv_far(n, lengths, occ, w1.T, w2)
    moved0, moved1 = [None] * n, [None] * n
    for k in far_of(n):
        moved0[k] = send(n, k, far0[k - n // 2])
    near = conv_near(n, lengths, cols2, w2s)
    moved0[0] = moved1[0] = near[0]
    for k in near_of(n):
        moved0[k] = moved1[k] = send(n, k, near[k])
    for k in far_of(n):
        moved1[k] = send(n, k, far1[k - n // 2])
    squares = jnp.zeros((8, C2), jnp.float32)
    first, squares = attend(n, 0, lengths, moved0, weights, squares, [])
    early = {k: send(n, k, first[k]) for k in far_of(n)}
    second, _ = attend(n, 1, lengths, moved1, weights, squares, list(first[: n // 2]))
    late = [second[0]] + [None] * (n - 1)
    for k in far_of(n) + near_of(n):
        late[k] = send(n, k, second[k])
    mine = tally(n, late)
    others = []
    for step in range(1, scenes):
        others.append(lax.ppermute(mine, "scene", [(i, i ^ step) for i in range(scenes)]))
    encoded = gather(n, frames, [early[k] for k in range(n // 2, n)], late)
    scale = 0.5 / float(scenes * n * frames * CELLS * C2)
    loss = finish(scale, mine, others)
    return (encoded[None], loss.reshape(()))


def solution(mesh):
    placed = (P("scene", "frame", None, None), P("scene"), P(), P(), P(), P(), P(), P(), P())
    return jax.shard_map(
        shards,
        mesh=mesh,
        in_specs=placed,
        out_specs=(P("scene", "frame", None, None), P()),
        check_vma=False,
    )
```
